128 devices in a mesh: ctx: 16 (over x, y), role: 2 (over z_hi), exp: 4 (over z_lo, core).
Axes of the slice: x: 4, y: 4, z: 4 (z_hi: 2, z_lo: 2; z = z_hi * 2 + z_lo), core: 2. Of those that a mesh axis runs over, the one named last changes fastest.
Arguments:
- queries: bfloat16 [2048, 32768], P('ctx', ('role', 'exp')), may hold values from -56 to 56
- latent: bfloat16 [2048, 512], P('ctx'), may hold values from -5 to 5
- frames: int32 [2048], replicated, may hold values from 0 to 31, never falling along the last dimension, each value on 1 to 128 neighbouring positions
- w_uv: bfloat16 [64, 512, 128], P(('role', 'exp')), may hold values from -0.5 to 0.5
- w_out: bfloat16 [8192, 7168], P(('role', 'exp'), 'ctx'), may hold values from -0.25 to 0.25
- residual: bfloat16 [2048, 7168], P('ctx', ('role', 'exp')), may hold values from -40 to 40
- norm_gain: float32 [7168], replicated, may hold values from 0.5 to 2
- expert_ids: int32 [2048, 2], P('ctx'), may hold values from 0 to 15, all different within a row; in each aligned block of 128 rows (0 to 127, 128 to 255, ...) at most 20 rows name the same one
- mix_codes: int32 [2048, 2], P('ctx'), may hold values from 1 to 256
- w_gate: bfloat16 [16, 7168, 1024], P('ctx', None, ('role', 'exp')), may hold values from -0.0625 to 0.0625
- w_up: bfloat16 [16, 7168, 1024], P('ctx', None, ('role', 'exp')), may hold values from -0.0625 to 0.0625
- w_down: bfloat16 [16, 1024, 7168], P('ctx', ('role', 'exp')), may hold values from -0.375 to 0.375
- grad_out: bfloat16 [2048, 7168], P('ctx', ('role', 'exp')), may hold values from -6 to 6
Outputs:
- layer_out: bfloat16 [2048, 7168], P('ctx', ('role', 'exp'))
- grad_pre_norm: bfloat16 [2048, 7168], P('ctx', ('role', 'exp'))
- grad_gate: bfloat16 [16, 7168, 1024], P('ctx', None, ('role', 'exp'))
- grad_up: bfloat16 [16, 7168, 1024], P('ctx', None, ('role', 'exp'))
- grad_down: bfloat16 [16, 1024, 7168], P('ctx', ('role', 'exp'))
The draws below stay inside these ranges and needn't reach their ends.
Inputs may be any that keep to these rules, and one draw needn't show every extreme that they name: `expert_ids`: each row names 2 different experts. Among the 128 rows of one index of ctx no expert is named more than 20 times, and in some such block one expert is named exactly 20 times. `frames`: never falls along the scene; each frame holds 1 to 128 tokens and one holds exactly 128.
All inputs are finite; a program needn't handle non-finite values.
Results may differ from the reference program's by a relative error of at most 0.03.
Values may be sent and summed in bfloat16 or wider, within the bound.
No kernel may reach another device: no remote copies, remote signals or barrier semaphores. Data moves between devices by JAX's collectives and lax.ppermute only.
A program may use at most 128 MiB of HBM per device.

```python
import math
import jax
import jax.numpy as jnp
import numpy as np
from jax import lax

D = 7168
DL = 512
DV = 128
HEADS = 64
FE = 1024
TOPK = 2
TOK_DEV = 128
GROUPS = 8
EXPERTS = 16
SEQ = 2048
CAP = 20
FRAMES = 32
N_CTX = 16


def scene_latent(key):
    latent_base = jnp.clip(jax.random.normal(jax.random.fold_in(key, 101), (SEQ, DL), jnp.float32), -4.5, 4.5)
    return latent_base


def draw_latent(key, part):
    latent_base = scene_latent(key)
    return latent_base.astype(jnp.bfloat16)


def draw_queries(key, part):
    query_draw = 1.5 * jnp.clip(jax.random.normal(jax.random.fold_in(key, 201), (SEQ, HEADS * DL), jnp.float32), -4.0, 4.0)
    return query_draw.astype(jnp.bfloat16)


def draw_residual(key, part):
    noise_draw = jnp.clip(jax.random.normal(jax.random.fold_in(key, 301), (SEQ, D), jnp.float32), -4.0, 4.0)
    row_scale = jnp.exp(jax.random.uniform(jax.random.fold_in(key, 302), (SEQ, 1), jnp.float32, math.log(0.25), math.log(2.5)))
    column_rise = math.log(3.0) * jnp.arange(D, dtype=jnp.float32) / (D - 1)
    column_scale = jnp.exp(column_rise[None, :] + jax.random.uniform(jax.random.fold_in(key, 303), (1, D), jnp.float32, -0.22, 0.22))
    return (noise_draw * row_scale * column_scale).astype(jnp.bfloat16)


def plant(array, key, smallest, high):
    longest = array.shape.index(max(array.shape))
    spots = []
    for shift in (0, 1):
        where = [jax.random.randint(jax.random.fold_in(key, axis), (), 0, length) for axis, length in enumerate(array.shape)]
        where[longest] = (where[longest] + shift) % array.shape[longest]
        spots.append(tuple(where))
    return array.at[spots[0]].set(smallest).at[spots[1]].set(high)


def level_of(rng, shape, shards, smallest, top_value):
    factor_of, own = 1.0, jax.random.fold_in(rng, 6)
    for axis_at, shards_of in shards:
        steps = jnp.exp(jax.random.uniform(jax.random.fold_in(own, axis_at), (shards_of,), jnp.float32, smallest / len(shards), top_value / len(shards)))
        factor_of = factor_of * jnp.repeat(steps, shape[axis_at] // shards_of).reshape([-1 if axis == axis_at else 1 for axis in range(len(shape))])
    return factor_of


def profile(number_of, total, limit, slope):
    weights = [(1 << 20) // math.isqrt(grade ** slope) + 1 for grade in range(2, number_of + 1)]
    surplus, holding = total - limit - (number_of - 1), [1] * (number_of - 1)
    while surplus > 0:
        free = [i for i in range(number_of - 1) if holding[i] < limit]
        pool, budget = sum([weights[i] for i in free]), surplus
        for i in free:
            more = min(limit - holding[i], max(1, budget * weights[i] // pool), surplus)
            holding[i] = holding[i] + more
            surplus = surplus - more
    return np.array([limit] + holding)


def uneven(key, number_of, total, bound, skew):
    if number_of == 2:
        one = jax.random.randint(key, (), max(1, total - bound), min(bound, total - 1) + 1)
        return jnp.stack([one, total - one])
    lengths = jnp.asarray(profile(number_of, total, bound, skew), jnp.int32)
    couples = (number_of - 1) // 2
    source_of, sink = lengths[1:1 + 2 * couples:2], lengths[2:2 + 2 * couples:2]
    slack = jnp.minimum(source_of - 1, bound - sink)
    passed = jax.random.randint(jax.random.fold_in(key, 1), (couples,), 0, 1 << 20) % (slack + 1)
    lengths = lengths.at[1:1 + 2 * couples:2].set(source_of - passed).at[2:2 + 2 * couples:2].set(sink + passed)
    return lengths[jax.random.permutation(jax.random.fold_in(key, 2), number_of)]


def deal_out(rng, own, number, rows, number_of, top, limit, slope):
    sequence = jax.random.permutation(rng, number_of)
    crowded, common = portions_of(number_of, rows * top, limit, slope, True), portions_of(number_of, rows * top, limit, slope, False)
    places = jnp.arange(number_of)

    def named(sizes, offset_by):
        used = int((sizes > 0).sum())
        fixed = max(1, used // 4)
        moved = fixed + (places - fixed + offset_by * (used - fixed)) % max(1, number_of - fixed)
        return jnp.zeros((number_of,), jnp.int32).at[sequence[jnp.where(places < fixed, places, moved)]].set(jnp.asarray(sizes, jnp.int32))

    sizes = jnp.where(number % 4 == 0, named(crowded, number // 4), named(common, number - number // 4 - 1))
    mixed = jax.random.permutation(jax.random.fold_in(own, 3), number_of)
    source_of, sink = mixed[0:number_of // 2 * 2:2], mixed[1:number_of // 2 * 2:2]
    room = jnp.minimum(sizes[source_of] - 1, limit - sizes[sink]) // 2
    room = jnp.where((source_of == sequence[0]) | (sink == sequence[0]) | (sizes[sink] == 0), 0, jnp.maximum(room, 0))
    moved = jax.random.randint(jax.random.fold_in(own, 4), (number_of // 2,), 0, 1 << 20) % (room + 1)
    sizes = sizes.at[source_of].add(-moved).at[sink].add(moved)
    items = jnp.searchsorted(jnp.cumsum(sizes), jnp.arange(rows * top), side="right").astype(jnp.int32)
    grid = items.reshape(top, rows).T
    grid = grid[jax.random.permutation(jax.random.fold_in(own, 1), rows)]
    offset_by = jax.random.randint(jax.random.fold_in(own, 2), (rows, 1), 0, top)
    return jnp.take_along_axis(grid, (jnp.arange(top)[None, :] + offset_by) % top, axis=1)


def portions_of(amount, total, limit, slope, full):
    portions = [(1 << 20) // math.isqrt(grade ** slope) + 1 for grade in range(1, amount + 1)]
    largest = limit if full else min(limit, max(-(-total // amount), total * portions[0] // sum(portions)))
    least = 1 if total - largest >= amount - 1 else 0
    holding, spare = [largest] + [least] * (amount - 1), total - largest - least * (amount - 1)
    while spare > 0:
        candidates = [i for i in range(1, amount) if holding[i] < largest] or [i for i in range(1, amount) if holding[i] < limit]
        mass, budget = sum([portions[i] for i in candidates]), spare
        for i in candidates:
            addition = min(limit - holding[i], max(1, budget * portions[i] // mass), spare)
            holding[i] = holding[i] + addition
            spare = spare - addition
    return np.array(holding)


def scatter_about(stream_key, extent, width, limit, cuts=(), kind=jnp.bfloat16):
    result = width * jax.random.normal(stream_key, extent, jnp.float32)
    if cuts:
        result = result * level_of(stream_key, extent, cuts, -0.22, 0.18)
    return jnp.clip(result, -limit, limit).astype(kind)


def setup_inputs(seed: int = 0) -> dict:
    splits = jax.random.split(jax.random.key(seed), 14)
    queries = draw_queries(jax.random.fold_in(splits[13], 71), 0)
    latent = draw_latent(jax.random.fold_in(splits[13], 71), 0)
    frames = jnp.searchsorted(jnp.cumsum(uneven(splits[2], FRAMES, SEQ, TOK_DEV, 1)), jnp.arange(SEQ), side="right").astype(jnp.int32)
    w_uv = scatter_about(splits[3], (HEADS, DL, DV), (DL // 4) ** -0.5, 0.5, ((0, 8),))
    w_out = scatter_about(splits[4], (HEADS * DV, D), (HEADS * DV // 16) ** -0.5, 0.25, ((0, 8), (1, 16)))
    residual = draw_residual(jax.random.fold_in(splits[13], 71), 0)
    norm_gain = jnp.clip(jnp.exp(jax.random.uniform(splits[6], (D,), jnp.float32, math.log(0.5), math.log(2.0))), 0.5, 2.0)
    expert_ids_keys = jax.random.split(jax.random.fold_in(splits[7], 1), SEQ // TOK_DEV)
    expert_ids_turns = jax.random.permutation(jax.random.fold_in(splits[7], 3), SEQ // TOK_DEV)
    expert_ids = jax.vmap(lambda own, number: deal_out(jax.random.fold_in(splits[7], 2), own, number, TOK_DEV, EXPERTS, TOPK, CAP, 2))(expert_ids_keys, expert_ids_turns).reshape((SEQ, TOPK))
    mix_codes = plant(jax.random.randint(splits[8], (SEQ, TOPK), 1, 257), jax.random.fold_in(splits[8], 1), 1, 256).astype(jnp.int32)
    w_gate = scatter_about(splits[9], (EXPERTS, D, FE), D ** -0.5, 0.0625, ((0, 16), (2, 8)))
    w_up = scatter_about(splits[10], (EXPERTS, D, FE), D ** -0.5, 0.0625, ((0, 16), (2, 8)))
    w_down = scatter_about(splits[11], (EXPERTS, FE, D), (FE // 4) ** -0.5, 0.375, ((0, 16), (1, 8)))
    grad_out = scatter_about(splits[12], (SEQ, D), 1.0, 6.0, ((0, 16), (1, 8)))
    return dict(queries=queries, latent=latent, frames=frames, w_uv=w_uv, w_out=w_out, residual=residual, norm_gain=norm_gain, expert_ids=expert_ids, mix_codes=mix_codes, w_gate=w_gate, w_up=w_up, w_down=w_down, grad_out=grad_out)


def settle(value):
    return lax.optimization_barrier(value.astype(jnp.bfloat16)).astype(jnp.float32)

def attend_head(query_head, latent, visible, uv_head):
    scores = jnp.dot(query_head, latent.T, preferred_element_type=jnp.float32) * DL ** (-0.5)
    scores = jnp.where(visible, scores, -1e+30)
    row_top = lax.optimization_barrier(jnp.max(scores, axis=-1, keepdims=True))
    exp_scores = jnp.exp(scores - row_top)
    attn_weights = (exp_scores / lax.optimization_barrier(jnp.sum(exp_scores, axis=-1, keepdims=True))).astype(jnp.bfloat16)
    latent_mix = jnp.dot(attn_weights, latent, preferred_element_type=jnp.float32).astype(jnp.bfloat16)
    return jnp.dot(latent_mix, uv_head, preferred_element_type=jnp.float32).astype(jnp.bfloat16)

def reference(queries, latent, frames, w_uv, w_out, residual, norm_gain, expert_ids, mix_codes, w_gate, w_up, w_down, grad_out):
    visible = frames[None, :] <= frames[:, None]
    per_head = jnp.transpose(queries.reshape(SEQ, HEADS, DL), (1, 0, 2))
    head_out = lax.map(lambda head_pair: attend_head(head_pair[0], latent, visible, head_pair[1]), (per_head, w_uv))
    head_out = jnp.transpose(head_out, (1, 0, 2)).reshape(SEQ, HEADS * DV)
    group_rows = HEADS * DV // GROUPS
    attn_sum = jnp.zeros((SEQ, D), jnp.float32)
    for group_index in range(GROUPS):
        lower = group_index * group_rows
        upper = lower + group_rows
        attn_sum = attn_sum + settle(jnp.dot(head_out[:, lower:upper], w_out[lower:upper], preferred_element_type=jnp.float32))
    pre_norm = (residual.astype(jnp.float32) + attn_sum).astype(jnp.bfloat16)
    pre_full = pre_norm.astype(jnp.float32)
    inv_scale = lax.rsqrt(lax.optimization_barrier(jnp.mean(pre_full * pre_full, axis=-1, keepdims=True)) + 1e-06)
    unit_rows = pre_full * inv_scale
    normed = (unit_rows * norm_gain).astype(jnp.bfloat16)
    code_values = mix_codes.astype(jnp.float32)
    mix_weight = code_values / lax.optimization_barrier(jnp.sum(code_values, axis=1, keepdims=True))
    mix_flat = mix_weight.reshape(-1)
    chosen = expert_ids.reshape(-1)
    pair_index = jnp.arange(SEQ * TOPK, dtype=jnp.int32)
    most_rows = N_CTX * CAP
    hidden_rows = FE // GROUPS

    def expert_pass(expert_item):
        expert, gate_weight, up_weight, down_weight = expert_item
        order_key = jnp.where(chosen == expert, pair_index, pair_index + SEQ * TOPK)
        row_order = jnp.argsort(order_key)[:most_rows].astype(jnp.int32)
        filled = chosen[row_order] == expert
        token_index = row_order // TOPK
        weight = jnp.where(filled, mix_flat[row_order], 0.0)
        expert_rows = jnp.where(filled[:, None], normed[token_index], jnp.zeros((), jnp.bfloat16))
        gate_in = jnp.dot(expert_rows, gate_weight, preferred_element_type=jnp.float32)
        up_in = jnp.dot(expert_rows, up_weight, preferred_element_type=jnp.float32)
        hidden = (jax.nn.silu(gate_in) * up_in).astype(jnp.bfloat16)
        down_total = jnp.zeros((most_rows, D), jnp.float32)
        for group_index in range(GROUPS):
            lower = group_index * hidden_rows
            upper = lower + hidden_rows
            down_total = down_total + settle(jnp.dot(hidden[:, lower:upper], down_weight[lower:upper], preferred_element_type=jnp.float32))
        expert_out = down_total.astype(jnp.bfloat16)
        out_grad = (weight[:, None] * grad_out[token_index].astype(jnp.float32)).astype(jnp.bfloat16)
        hidden_grad = jnp.dot(out_grad, down_weight.T, preferred_element_type=jnp.float32)
        gate_sig = jax.nn.sigmoid(gate_in)
        gate_grad = (hidden_grad * up_in * gate_sig * (1.0 + gate_in * (1.0 - gate_sig))).astype(jnp.bfloat16)
        up_grad = (hidden_grad * jax.nn.silu(gate_in)).astype(jnp.bfloat16)
        grad_down = jnp.dot(hidden.T, out_grad, preferred_element_type=jnp.float32).astype(jnp.bfloat16)
        grad_gate = jnp.dot(expert_rows.T, gate_grad, preferred_element_type=jnp.float32).astype(jnp.bfloat16)
        grad_up = jnp.dot(expert_rows.T, up_grad, preferred_element_type=jnp.float32).astype(jnp.bfloat16)
        grad_total = jnp.zeros((most_rows, D), jnp.float32)
        for group_index in range(GROUPS):
            lower = group_index * hidden_rows
            upper = lower + hidden_rows
            gate_part = jnp.dot(gate_grad[:, lower:upper], gate_weight[:, lower:upper].T, preferred_element_type=jnp.float32)
            up_part = jnp.dot(up_grad[:, lower:upper], up_weight[:, lower:upper].T, preferred_element_type=jnp.float32)
            grad_total = grad_total + settle(gate_part + up_part)
        row_grad = grad_total.astype(jnp.bfloat16)
        return (token_index, weight, expert_out, row_grad, grad_gate, grad_up, grad_down)
    experts_range = jnp.arange(EXPERTS, dtype=jnp.int32)
    token_all, weight_all, out_all, grad_all, grad_gate, grad_up, grad_down = lax.map(expert_pass, (experts_range, w_gate, w_up, w_down))
    flat_tokens = token_all.reshape(-1)
    routed = jnp.zeros((SEQ, D), jnp.float32).at[flat_tokens].add(weight_all.reshape(-1)[:, None] * out_all.reshape(-1, D).astype(jnp.float32))
    layer_out = (pre_full + routed).astype(jnp.bfloat16)
    normed_grad = jnp.zeros((SEQ, D), jnp.float32).at[flat_tokens].add(grad_all.reshape(-1, D).astype(jnp.float32)).astype(jnp.bfloat16)
    scaled_grad = normed_grad.astype(jnp.float32) * norm_gain
    center = lax.optimization_barrier(jnp.mean(scaled_grad * unit_rows, axis=-1, keepdims=True))
    grad_pre_norm = (grad_out.astype(jnp.float32) + inv_scale * (scaled_grad - unit_rows * center)).astype(jnp.bfloat16)
    return (layer_out, grad_pre_norm, grad_gate, grad_up, grad_down)
```

```python
import jax
import jax.numpy as jnp
from jax import lax
from jax.sharding import PartitionSpec as P

ALL = ("ctx", "role", "exp")
GROUP = ("role", "exp")
BF16 = jnp.bfloat16
F32 = jnp.float32
SIDE = 4


def dot(a, b, dims=((1,), (0,))):
    return lax.dot_general(a, b, (dims, ((), ())), preferred_element_type=F32)


def shift_z(block, step):
    return lax.ppermute(block, GROUP, [(g, (g + 2 * step) % 8) for g in range(8)])


def swap_core(block):
    return lax.ppermute(block, GROUP, [(g, g ^ 1) for g in range(8)])


def shift_plane(block, phase, step):
    pairs = []
    for c in range(SIDE * SIDE):
        x, y = divmod(c, SIDE)
        for g in range(8):
            if g % 2 == phase:
                to = x * SIDE + (y + step) % SIDE
            else:
                to = (x + step) % SIDE * SIDE + y
            pairs.append((c * 8 + g, to * 8 + g))
    return lax.ppermute(block, ALL, pairs)


def ring_gather(block, shift):
    half = block.shape[0] // 2
    before = shift(block, 1)
    after = shift(block, -1)
    far = jnp.concatenate([shift(before[:half], 1), shift(after[half:], -1)], 0)
    return jnp.stack([block, after, far, before])


def ctx_gather(block):
    first = ring_gather(block, lambda b, s: shift_plane(b, 0, s))
    return ring_gather(first, lambda b, s: shift_plane(b, 1, s))


def group_gather(block):
    rows = ring_list(block)
    return [part for own in rows for part in (own, swap_core(own))]


def ring_list(block):
    half = block.shape[0] // 2
    before = shift_z(block, 1)
    after = shift_z(block, -1)
    far = jnp.concatenate([shift_z(before[:half], 1), shift_z(after[half:], -1)], 0)
    return [block, after, far, before]


def group_exchange(blocks, place_z, core):
    by_core = blocks.reshape(SIDE, 2, *blocks.shape[1:])
    keep = lax.dynamic_index_in_dim(by_core, core, 1, False)
    give = lax.dynamic_index_in_dim(by_core, 1 - core, 1, False)
    both = jnp.stack([keep, swap_core(give)], 1)

    def bound_for(step):
        return lax.dynamic_index_in_dim(both, (place_z + step) % SIDE, 0, False)

    received = [
        bound_for(0),
        shift_z(bound_for(3), -1),
        shift_z(bound_for(2), 2),
        shift_z(bound_for(1), 1),
    ]
    return jnp.concatenate(received, 0)


def roll_lead(array, shift, axis):
    twice = jnp.concatenate([array, array], axis)
    return lax.dynamic_slice_in_dim(twice, shift, SIDE, axis)


def split3(value):
    high = lax.reduce_precision(value, 8, 7)
    rest = value - high
    middle = lax.reduce_precision(rest, 8, 7)
    low = lax.reduce_precision(rest - middle, 8, 7)
    return [term.astype(BF16) for term in (high, middle, low)]


def pad_lanes(terms):
    rows = terms[0].shape[0]
    blank = jnp.zeros((rows, 128 - len(terms)), BF16)
    return jnp.concatenate([t.reshape(rows, 1) for t in terms] + [blank], 1)


def per_device(
    queries,
    latent,
    frames,
    w_uv,
    w_out,
    residual,
    norm_gain,
    expert_ids,
    mix_codes,
    w_gate,
    w_up,
    w_down,
    grad_out,
):
    ctx_count = lax.axis_size("ctx")
    ctx_place = lax.axis_index("ctx")
    plane_x, plane_y = ctx_place // SIDE, ctx_place % SIDE
    group_place = lax.axis_index(GROUP)
    place_z, core = group_place // 2, group_place % 2
    group_count = 8
    token_count = queries.shape[0]
    head_count, latent_width, value_width = w_uv.shape
    model_width = w_gate.shape[1]
    slice_width = residual.shape[1]
    top_count = expert_ids.shape[1]
    hidden_width = w_gate.shape[2]
    column_width = w_out.shape[1]
    part_tokens = token_count // group_count
    capacity = token_count * top_count // ctx_count * 5 // 4
    slot_total = ctx_count * capacity

    out_weight = lax.all_gather(w_out, GROUP, axis=0, tiled=True)
    weight_blocks = jnp.concatenate(
        [
            jnp.transpose(w_down[0].reshape(hidden_width, group_count, slice_width), (1, 0, 2)),
            jnp.transpose(w_gate[0].reshape(group_count, slice_width, hidden_width), (0, 2, 1)),
            jnp.transpose(w_up[0].reshape(group_count, slice_width, hidden_width), (0, 2, 1)),
        ],
        1,
    )
    slice_weights = group_exchange(weight_blocks, place_z, core)
    residual_part = lax.all_to_all(
        residual.reshape(group_count, part_tokens, slice_width), GROUP, 0, 0, tiled=True
    )
    residual_part = jnp.transpose(residual_part, (1, 0, 2)).reshape(part_tokens, model_width)

    chosen = expert_ids.reshape(-1)
    pair_range = jnp.arange(token_count * top_count, dtype=jnp.int32)
    same = (chosen[:, None] == chosen[None, :]) & (pair_range[None, :] < pair_range[:, None])
    earlier = jnp.sum(same.astype(jnp.int32), axis=1)
    slot_index = (chosen * capacity + earlier).reshape(token_count, top_count)
    slot_range = jnp.arange(slot_total, dtype=jnp.int32)
    code_values = mix_codes.astype(F32)
    mix_weight = code_values / jnp.sum(code_values, axis=1, keepdims=True)
    hits = [slot_index[:, k][None, :] == slot_range[:, None] for k in range(top_count)]
    pick = sum(hit.astype(F32) for hit in hits).astype(BF16)
    slot_weight = sum(
        jnp.sum(jnp.where(hits[k], mix_weight[:, k][None, :], 0.0), axis=1) for k in range(top_count)
    )
    returns = [
        (slot_index[:, k][:, None] == slot_range[None, :]).astype(BF16) for k in range(top_count)
    ]

    def to_experts(rows):
        return lax.all_to_all(rows, "ctx", split_axis=0, concat_axis=0, tiled=True)

    grad_rows = (dot(pick, grad_out) * slot_weight[:, None]).astype(BF16)
    out_grad = lax.all_gather(to_experts(grad_rows), GROUP, axis=1, tiled=True)

    half = token_count // 2
    own_keys = ctx_gather(lax.dynamic_slice_in_dim(latent, core * half, half, 0))
    own_keys = own_keys.reshape(ctx_count * half, latent_width)
    key_rows = jnp.concatenate([own_keys, swap_core(own_keys)], 0)
    own_frames = lax.dynamic_slice_in_dim(frames, ctx_place * token_count, token_count)
    frame_grid = frames.reshape(SIDE, SIDE, 2, half)
    frame_grid = roll_lead(roll_lead(frame_grid, plane_x, 0), plane_y, 1)
    by_x = jnp.transpose(frame_grid, (2, 0, 1, 3))
    by_y = jnp.transpose(frame_grid, (2, 1, 0, 3))
    key_frames = jnp.where(
        core == 0,
        jnp.concatenate([by_x[0].reshape(-1), by_y[1].reshape(-1)]),
        jnp.concatenate([by_y[1].reshape(-1), by_x[0].reshape(-1)]),
    )
    visible = key_frames[None, :] <= own_frames[:, None]
    query_heads = queries.reshape(token_count, head_count, latent_width)
    scores = jnp.einsum(
        "thd,sd->hts", query_heads, key_rows, preferred_element_type=F32
    ) * latent_width ** (-0.5)
    scores = jnp.where(visible[None, :, :], scores, -1e30)
    row_top = jnp.max(scores, axis=-1, keepdims=True)
    exp_scores = jnp.exp(scores - row_top)
    attn_weights = (exp_scores / jnp.sum(exp_scores, axis=-1, keepdims=True)).astype(BF16)
    latent_mix = jnp.einsum(
        "hts,sd->thd", attn_weights, key_rows, preferred_element_type=F32
    ).astype(BF16)
    head_out = jnp.einsum("thd,hdv->thv", latent_mix, w_uv, preferred_element_type=F32).astype(BF16)
    head_out = head_out.reshape(group_count, part_tokens, head_count * value_width)

    head_part = lax.all_to_all(head_out, GROUP, 0, 0, tiled=True)
    head_part = jnp.transpose(head_part, (1, 0, 2)).reshape(part_tokens, -1)
    all_heads = ctx_gather(head_part).reshape(ctx_count * part_tokens, -1)
    columns = dot(all_heads, out_weight).astype(BF16)
    columns = columns.reshape(SIDE, SIDE, part_tokens, column_width)
    columns = jnp.where(core == 0, columns, jnp.transpose(columns, (1, 0, 2, 3)))
    columns = roll_lead(roll_lead(columns, (SIDE - plane_x) % SIDE, 0), (SIDE - plane_y) % SIDE, 1)
    columns = to_experts(columns.reshape(ctx_count, part_tokens, column_width))
    attn_part = jnp.transpose(columns, (1, 0, 2)).reshape(part_tokens, model_width)
    pre_part = (residual_part.astype(F32) + attn_part.astype(F32)).astype(BF16)
    pre_wide = pre_part.astype(F32)
    inv_part = lax.rsqrt(jnp.mean(pre_wide * pre_wide, axis=-1, keepdims=True) + 1e-06)
    inv_lanes = pad_lanes(split3(inv_part))
    pre_send = jnp.concatenate(
        [
            jnp.transpose(pre_part.reshape(part_tokens, group_count, slice_width), (1, 0, 2)),
            jnp.broadcast_to(inv_lanes[None], (group_count, part_tokens, 128)),
        ],
        2,
    )
    pre_back = lax.all_to_all(pre_send, GROUP, 0, 0, tiled=True).reshape(token_count, -1)
    pre_norm = pre_back[:, :slice_width].astype(F32)
    inv_scale = jnp.sum(pre_back[:, slice_width : slice_width + 3].astype(F32), axis=1, keepdims=True)
    unit_rows = pre_norm * inv_scale
    local_gain = lax.dynamic_slice_in_dim(norm_gain, group_place * slice_width, slice_width)
    normed = (unit_rows * local_gain).astype(BF16)

    expert_rows = lax.all_gather(
        to_experts(dot(pick, normed).astype(BF16)), GROUP, axis=1, tiled=True
    )
    gate_weight, up_weight, down_weight = w_gate[0], w_up[0], w_down[0]
    gate_in = dot(expert_rows, gate_weight)
    up_in = dot(expert_rows, up_weight)
    gate_sig = jax.nn.sigmoid(gate_in)
    silu = gate_in * gate_sig
    hidden = (silu * up_in).astype(BF16)
    hidden_grad = dot(out_grad, down_weight, ((1,), (1,)))
    gate_wide = hidden_grad * up_in * gate_sig * (1.0 + gate_in * (1.0 - gate_sig))
    up_wide = hidden_grad * silu
    gate_grad = gate_wide.astype(BF16)
    up_grad = up_wide.astype(BF16)
    center_part = jnp.sum(gate_wide * gate_in + up_wide * up_in, axis=1, keepdims=True)
    grad_down = dot(hidden, out_grad, ((0,), (0,))).astype(BF16)[None]
    grad_gate = dot(expert_rows, gate_grad, ((0,), (0,))).astype(BF16)[None]
    grad_up = dot(expert_rows, up_grad, ((0,), (0,))).astype(BF16)[None]
    hidden_send = jnp.concatenate([hidden, gate_grad, up_grad, pad_lanes(split3(center_part))], 1)
    members = group_gather(hidden_send)
    rows_out = 0.0
    row_grad = 0.0
    center_slot = 0.0
    for place, member in enumerate(members):
        weights = slice_weights[place]
        rows_out = rows_out + dot(member[:, :hidden_width], weights[:hidden_width])
        row_grad = row_grad + dot(
            member[:, hidden_width : 3 * hidden_width], weights[hidden_width:]
        )
        center_slot = center_slot + jnp.sum(
            member[:, 3 * hidden_width : 3 * hidden_width + 3].astype(F32), axis=1, keepdims=True
        )
    back = jnp.concatenate(
        [rows_out.astype(BF16), row_grad.astype(BF16), pad_lanes(split3(center_slot))], 1
    )
    back = to_experts(back)

    routed = sum(
        dot(returns[k], back[:, :slice_width]) * mix_weight[:, k : k + 1] for k in range(top_count)
    )
    layer_out = (pre_norm + routed).astype(BF16)
    summed = dot(returns[0] + returns[1], back[:, slice_width:])
    normed_grad = summed[:, :slice_width].astype(BF16).astype(F32)
    center = jnp.sum(summed[:, slice_width : slice_width + 3], axis=1, keepdims=True) / model_width
    scaled_grad = normed_grad * local_gain
    grad_pre_norm = (
        grad_out.astype(F32) + inv_scale * (scaled_grad - unit_rows * center)
    ).astype(BF16)
    return (layer_out, grad_pre_norm, grad_gate, grad_up, grad_down)


def solution(mesh):
    placed = (
        P("ctx", ("role", "exp")),
        P("ctx", None),
        P(),
        P(("role", "exp"), None, None),
        P(("role", "exp"), "ctx"),
        P("ctx", ("role", "exp")),
        P(),
        P("ctx", None),
        P("ctx", None),
        P("ctx", None, ("role", "exp")),
        P("ctx", None, ("role", "exp")),
        P("ctx", ("role", "exp"), None),
        P("ctx", ("role", "exp")),
    )
    return jax.shard_map(
        per_device,
        mesh=mesh,
        in_specs=placed,
        out_specs=(
            P("ctx", ("role", "exp")),
            P("ctx", ("role", "exp")),
            P("ctx", None, ("role", "exp")),
            P("ctx", None, ("role", "exp")),
            P("ctx", ("role", "exp"), None),
        ),
        check_vma=False,
    )
```

```python
import functools

import jax
import jax.numpy as jnp
from jax import lax
from jax.experimental import pallas as pl
from jax.experimental.pallas import tpu as pltpu
from jax.sharding import PartitionSpec as P

ALL = ("ctx", "role", "exp")
GROUP = ("role", "exp")
BF16 = jnp.bfloat16
F32 = jnp.float32
SIDE = 4
LANES = 128


def dot(a, b, dims=((1,), (0,))):
    return lax.dot_general(a, b, (dims, ((), ())), preferred_element_type=F32)


def shift_z(block, step):
    return lax.ppermute(block, GROUP, [(g, (g + 2 * step) % 8) for g in range(8)])


def swap_core(block):
    return lax.ppermute(block, GROUP, [(g, g ^ 1) for g in range(8)])


def shift_plane(block, phase, step):
    pairs = []
    for c in range(SIDE * SIDE):
        x, y = divmod(c, SIDE)
        for g in range(8):
            if g % 2 == phase:
                to = x * SIDE + (y + step) % SIDE
            else:
                to = (x + step) % SIDE * SIDE + y
            pairs.append((c * 8 + g, to * 8 + g))
    return lax.ppermute(block, ALL, pairs)


def ring_list(block, shift):
    half = block.shape[0] // 2
    before = shift(block, 1)
    after = shift(block, -1)
    far = [shift(before[:half], 1), shift(after[half:], -1)]
    return [block, after, jnp.concatenate(far, 0), before]


def ctx_gather(block):
    first = ring_list(block, lambda b, s: shift_plane(b, 0, s))
    first = jnp.stack(first)
    return ring_list(first, lambda b, s: shift_plane(b, 1, s))


def group_gather(block):
    rows = ring_list(block, shift_z)
    return [part for own in rows for part in (own, swap_core(own))]


def group_exchange(blocks):
    received = [
        blocks[0],
        shift_z(blocks[3], -1),
        shift_z(blocks[2], 2),
        shift_z(blocks[1], 1),
    ]
    return [part for pair in received for part in (pair[0], swap_core(pair[1]))]


def roll_lead(array, shift, axis):
    twice = jnp.concatenate([array, array], axis)
    return lax.dynamic_slice_in_dim(twice, shift, SIDE, axis)


def split3(value):
    high = lax.reduce_precision(value, 8, 7)
    rest = value - high
    middle = lax.reduce_precision(rest, 8, 7)
    low = lax.reduce_precision(rest - middle, 8, 7)
    return [term.astype(BF16) for term in (high, middle, low)]


def pad_lanes(terms):
    rows = terms[0].shape[0]
    blank = jnp.zeros((rows, LANES - len(terms)), BF16)
    return jnp.concatenate([t.reshape(rows, 1) for t in terms] + [blank], 1)


def lanes3(value):
    lane = lax.broadcasted_iota(jnp.int32, (value.shape[0], LANES), 1)
    high = value.astype(BF16).astype(F32)
    rest = value - high
    middle = rest.astype(BF16).astype(F32)
    low = rest - middle
    wide = jnp.where(lane == 0, high, jnp.where(lane == 1, middle, jnp.where(lane == 2, low, 0.0)))
    return wide.astype(BF16)


def call(kernel, outs, scalars=0, **params):
    def run(*operands):
        spaces = [pltpu.SMEM] * scalars + [pltpu.VMEM] * (len(operands) - scalars)
        return pl.pallas_call(
            kernel,
            out_shape=outs,
            in_specs=[pl.BlockSpec(memory_space=space) for space in spaces],
            **params,
        )(*operands)

    return run


def prepare_kernel(place_ref, down_ref, gate_ref, up_ref, *outs):
    rows_ref = outs[SIDE]
    slice_width = rows_ref.shape[1]
    hidden = down_ref.shape[0]
    for step in range(SIDE):
        for other in range(2):
            z = lax.rem(place_ref[0] + step, SIDE)
            core = place_ref[1] + other - 2 * place_ref[1] * other
            start = pl.multiple_of((2 * z + core) * slice_width, LANES)
            gate = gate_ref[pl.ds(start, slice_width), :]
            up = up_ref[pl.ds(start, slice_width), :]
            outs[step][other, :, :hidden] = down_ref[:, pl.ds(start, slice_width)].T
            outs[step][other, :, hidden : 2 * hidden] = gate
            outs[step][other, :, 2 * hidden :] = up
            rows_ref[2 * step + other, :, :hidden] = gate
            rows_ref[2 * step + other, :, hidden:] = up


def attend_kernel(scale, q_ref, near_ref, far_ref, key_frame_ref, own_frame_ref, uv_ref, out_ref):
    heads, latent_width, value_width = uv_ref.shape
    tokens = q_ref.shape[0]
    keys = [near_ref[...], far_ref[...]]
    count = keys[0].shape[0]
    query = jnp.concatenate(
        [q_ref[:, h * latent_width : (h + 1) * latent_width] for h in range(heads)], 0
    )
    own = own_frame_ref[...]
    scores = []
    for part in range(2):
        visible = key_frame_ref[:, part * count : (part + 1) * count] <= own
        visible = jnp.concatenate([visible.astype(F32)] * heads, 0) > 0.5
        scores.append(jnp.where(visible, dot(query, keys[part], ((1,), (1,))) * scale, -1e30))
    top = jnp.maximum(*[jnp.max(s, axis=1, keepdims=True) for s in scores])
    weights = [jnp.exp(s - top) for s in scores]
    total = sum(jnp.sum(w, axis=1, keepdims=True) for w in weights)
    mix = sum(dot(w.astype(BF16), k) for w, k in zip(weights, keys))
    mix = (mix / total).astype(BF16)
    for h in range(heads):
        out_ref[:, h * value_width : (h + 1) * value_width] = dot(
            mix[h * tokens : (h + 1) * tokens], uv_ref[h]
        ).astype(BF16)


def expert_kernel(*refs):
    row_refs, weight_ref, back_ref, out_ref = refs[:8], refs[8], refs[9], refs[10]
    both = dot(row_refs[0][...], weight_ref[0])
    for place in range(1, 8):
        both = both + dot(row_refs[place][...], weight_ref[place])
    hidden = both.shape[1] // 2
    gate_in, up_in = both[:, :hidden], both[:, hidden:]
    hidden_grad = back_ref[...]
    gate_sig = 1.0 / (1.0 + jnp.exp(-gate_in))
    silu = gate_in * gate_sig
    gate_grad = hidden_grad * up_in * gate_sig * (1.0 + gate_in * (1.0 - gate_sig))
    up_grad = hidden_grad * silu
    center = jnp.sum(gate_grad * gate_in + up_grad * up_in, axis=1, keepdims=True)
    out_ref[:, :hidden] = (silu * up_in).astype(BF16)
    out_ref[:, hidden : 2 * hidden] = gate_grad.astype(BF16)
    out_ref[:, 2 * hidden : 3 * hidden] = up_grad.astype(BF16)
    out_ref[:, 3 * hidden :] = lanes3(center)


def weight_grad_kernel(place_ref, *refs):
    row_refs, hidden_ref, gate_ref, up_ref = refs[:8], refs[8], refs[9], refs[10]
    hidden = gate_ref.shape[1]
    slice_width = row_refs[0].shape[1]
    grads = hidden_ref[:, hidden : 3 * hidden]
    for step in range(SIDE):
        for other in range(2):
            z = lax.rem(place_ref[0] + step, SIDE)
            core = place_ref[1] + other - 2 * place_ref[1] * other
            start = pl.multiple_of((2 * z + core) * slice_width, LANES)
            both = dot(row_refs[2 * step + other][...], grads, ((0,), (0,)))
            gate_ref[pl.ds(start, slice_width), :] = both[:, :hidden].astype(BF16)
            up_ref[pl.ds(start, slice_width), :] = both[:, hidden:].astype(BF16)


def project_kernel(*refs):
    member_refs, weight_refs, out_ref = refs[:8], refs[8:16], refs[16]
    slice_width, wide = weight_refs[0].shape
    hidden = wide // 3
    rows, grads, center = 0.0, 0.0, 0.0
    for member_ref, weight_ref in zip(member_refs, weight_refs):
        rows = rows + dot(member_ref[:, :hidden], weight_ref[:, :hidden], ((1,), (1,)))
        grads = grads + dot(
            member_ref[:, hidden : 3 * hidden], weight_ref[:, hidden:], ((1,), (1,))
        )
        center = center + jnp.sum(member_ref[:, 3 * hidden :].astype(F32), axis=1, keepdims=True)
    out_ref[:, :slice_width] = rows.astype(BF16)
    out_ref[:, slice_width : 2 * slice_width] = grads.astype(BF16)
    out_ref[:, 2 * slice_width :] = lanes3(center)


def per_device(
    queries,
    latent,
    frames,
    w_uv,
    w_out,
    residual,
    norm_gain,
    expert_ids,
    mix_codes,
    w_gate,
    w_up,
    w_down,
    grad_out,
):
    ctx_count = lax.axis_size("ctx")
    ctx_place = lax.axis_index("ctx")
    plane_x, plane_y = ctx_place // SIDE, ctx_place % SIDE
    group_place = lax.axis_index(GROUP)
    place_z, core = group_place // 2, group_place % 2
    group_count = 8
    token_count = queries.shape[0]
    head_count, latent_width, value_width = w_uv.shape
    model_width = w_gate.shape[1]
    slice_width = residual.shape[1]
    top_count = expert_ids.shape[1]
    hidden_width = w_gate.shape[2]
    column_width = w_out.shape[1]
    part_tokens = token_count // group_count
    capacity = token_count * top_count // ctx_count * 5 // 4
    slot_total = ctx_count * capacity

    def shape(*dims):
        return jax.ShapeDtypeStruct(dims, BF16)

    places = jnp.stack([place_z, core]).astype(jnp.int32)

    out_weight = lax.all_gather(w_out, GROUP, axis=0, tiled=True)
    *weight_blocks, row_weights = call(
        prepare_kernel,
        [shape(2, slice_width, 3 * hidden_width)] * SIDE
        + [shape(group_count, slice_width, 2 * hidden_width)],
        1,
    )(places, w_down[0], w_gate[0], w_up[0])
    slice_weights = group_exchange(weight_blocks)

    shares = residual.reshape(SIDE, 2, part_tokens, slice_width)
    shares = roll_lead(shares, place_z, 0)
    shares = jnp.where(core == 0, shares, shares[:, ::-1])
    shares = group_exchange([shares[i] for i in range(SIDE)])
    shares = jnp.stack(shares).reshape(SIDE, 2, part_tokens, slice_width)
    shares = jnp.where(core == 0, shares, shares[:, ::-1])
    shares = roll_lead(shares, (SIDE - place_z) % SIDE, 0)
    residual_part = jnp.transpose(
        shares.reshape(group_count, part_tokens, slice_width), (1, 0, 2)
    ).reshape(part_tokens, model_width)

    chosen = expert_ids.reshape(-1)
    pair_range = jnp.arange(token_count * top_count, dtype=jnp.int32)
    same = (chosen[:, None] == chosen[None, :]) & (pair_range[None, :] < pair_range[:, None])
    earlier = jnp.sum(same.astype(jnp.int32), axis=1)
    slot_index = (chosen * capacity + earlier).reshape(token_count, top_count)
    slot_range = jnp.arange(slot_total, dtype=jnp.int32)
    code_values = mix_codes.astype(F32)
    mix_weight = code_values / jnp.sum(code_values, axis=1, keepdims=True)
    hits = [slot_index[:, k][None, :] == slot_range[:, None] for k in range(top_count)]
    pick = sum(hit.astype(F32) for hit in hits).astype(BF16)
    slot_weight = sum(
        jnp.sum(jnp.where(hits[k], mix_weight[:, k][None, :], 0.0), axis=1) for k in range(top_count)
    )
    returns = [
        (slot_index[:, k][:, None] == slot_range[None, :]).astype(BF16) for k in range(top_count)
    ]

    def to_experts(rows):
        return lax.all_to_all(rows, "ctx", split_axis=0, concat_axis=0, tiled=True)

    grad_rows = (dot(pick, grad_out) * slot_weight[:, None]).astype(BF16)
    out_grad = lax.all_gather(to_experts(grad_rows), GROUP, axis=1, tiled=True)

    half = token_count // 2
    own_keys = ctx_gather(lax.dynamic_slice_in_dim(latent, core * half, half, 0))
    own_keys = jnp.stack(own_keys).reshape(ctx_count * half, latent_width)
    other_keys = swap_core(own_keys)
    own_frames = lax.dynamic_slice_in_dim(frames, ctx_place * token_count, token_count)
    frame_grid = frames.reshape(SIDE, SIDE, 2, half)
    frame_grid = roll_lead(roll_lead(frame_grid, plane_x, 0), plane_y, 1)
    by_x = jnp.transpose(frame_grid, (2, 0, 1, 3))
    by_y = jnp.transpose(frame_grid, (2, 1, 0, 3))
    key_frames = jnp.where(
        core == 0,
        jnp.concatenate([by_x[0].reshape(-1), by_y[1].reshape(-1)]),
        jnp.concatenate([by_y[1].reshape(-1), by_x[0].reshape(-1)]),
    )
    heads = 2
    head_out = pl.pallas_call(
        functools.partial(attend_kernel, latent_width ** (-0.5)),
        out_shape=shape(token_count, head_count * value_width),
        grid=(head_count // heads,),
        in_specs=[
            pl.BlockSpec((token_count, heads * latent_width), lambda h: (0, h)),
            pl.BlockSpec(own_keys.shape, lambda h: (0, 0)),
            pl.BlockSpec(other_keys.shape, lambda h: (0, 0)),
            pl.BlockSpec((1, ctx_count * token_count), lambda h: (0, 0)),
            pl.BlockSpec((token_count, 1), lambda h: (0, 0)),
            pl.BlockSpec((heads, latent_width, value_width), lambda h: (h, 0, 0)),
        ],
        out_specs=pl.BlockSpec((token_count, heads * value_width), lambda h: (0, h)),
        name="attend",
    )(queries, own_keys, other_keys, key_frames[None], own_frames[:, None], w_uv)
    head_out = head_out.reshape(group_count, part_tokens, head_count * value_width)

    head_part = lax.all_to_all(head_out, GROUP, 0, 0, tiled=True)
    head_part = jnp.transpose(head_part, (1, 0, 2)).reshape(part_tokens, -1)
    all_heads = jnp.stack(ctx_gather(head_part)).reshape(ctx_count * part_tokens, -1)
    columns = dot(all_heads, out_weight).astype(BF16)
    columns = columns.reshape(SIDE, SIDE, part_tokens, column_width)
    columns = jnp.where(core == 0, columns, jnp.transpose(columns, (1, 0, 2, 3)))
    columns = roll_lead(roll_lead(columns, (SIDE - plane_x) % SIDE, 0), (SIDE - plane_y) % SIDE, 1)
    columns = to_experts(columns.reshape(ctx_count, part_tokens, column_width))
    attn_part = jnp.transpose(columns, (1, 0, 2)).reshape(part_tokens, model_width)
    pre_part = (residual_part.astype(F32) + attn_part.astype(F32)).astype(BF16)
    pre_wide = pre_part.astype(F32)
    inv_part = lax.rsqrt(jnp.mean(pre_wide * pre_wide, axis=-1, keepdims=True) + 1e-06)
    inv_lanes = pad_lanes(split3(inv_part))
    pre_send = jnp.concatenate(
        [
            jnp.transpose(pre_part.reshape(part_tokens, group_count, slice_width), (1, 0, 2)),
            jnp.broadcast_to(inv_lanes[None], (group_count, part_tokens, 128)),
        ],
        2,
    )
    pre_back = lax.all_to_all(pre_send, GROUP, 0, 0, tiled=True).reshape(token_count, -1)
    pre_norm = pre_back[:, :slice_width].astype(F32)
    inv_scale = jnp.sum(pre_back[:, slice_width : slice_width + 3].astype(F32), axis=1, keepdims=True)
    unit_rows = pre_norm * inv_scale
    local_gain = lax.dynamic_slice_in_dim(norm_gain, group_place * slice_width, slice_width)
    normed = (unit_rows * local_gain).astype(BF16)

    expert_rows = group_gather(to_experts(dot(pick, normed).astype(BF16)))
    hidden_grad = dot(out_grad, w_down[0], ((1,), (1,)))
    hidden_send = call(expert_kernel, shape(slot_total, 3 * hidden_width + LANES))(
        *expert_rows, row_weights, hidden_grad
    )
    members = group_gather(hidden_send)
    grad_gate, grad_up = call(
        weight_grad_kernel, [shape(model_width, hidden_width)] * 2, 1
    )(places, *expert_rows, hidden_send)
    grad_gate, grad_up = grad_gate[None], grad_up[None]
    grad_down = dot(hidden_send[:, :hidden_width], out_grad, ((0,), (0,))).astype(BF16)[None]
    back = call(project_kernel, shape(slot_total, 2 * slice_width + LANES))(
        *members, *slice_weights
    )
    back = to_experts(back)

    routed = sum(
        dot(returns[k], back[:, :slice_width]) * mix_weight[:, k : k + 1] for k in range(top_count)
    )
    layer_out = (pre_norm + routed).astype(BF16)
    summed = dot(returns[0] + returns[1], back[:, slice_width:])
    normed_grad = summed[:, :slice_width].astype(BF16).astype(F32)
    center = jnp.sum(summed[:, slice_width : slice_width + 3], axis=1, keepdims=True) / model_width
    scaled_grad = normed_grad * local_gain
    grad_pre_norm = (
        grad_out.astype(F32) + inv_scale * (scaled_grad - unit_rows * center)
    ).astype(BF16)
    return (layer_out, grad_pre_norm, grad_gate, grad_up, grad_down)


def solution(mesh):
    placed = (
        P("ctx", ("role", "exp")),
        P("ctx", None),
        P(),
        P(("role", "exp"), None, None),
        P(("role", "exp"), "ctx"),
        P("ctx", ("role", "exp")),
        P(),
        P("ctx", None),
        P("ctx", None),
        P("ctx", None, ("role", "exp")),
        P("ctx", None, ("role", "exp")),
        P("ctx", ("role", "exp"), None),
        P("ctx", ("role", "exp")),
    )

    return jax.shard_map(
        per_device,
        mesh=mesh,
        in_specs=placed,
        out_specs=(
            P("ctx", ("role", "exp")),
            P("ctx", ("role", "exp")),
            P("ctx", None, ("role", "exp")),
            P("ctx", None, ("role", "exp")),
            P("ctx", ("role", "exp"), None),
        ),
        check_vma=False,
    )
```

```python
import functools

import jax
import jax.numpy as jnp
from jax import lax
from jax.experimental import pallas as pl
from jax.experimental.pallas import tpu as pltpu
from jax.sharding import PartitionSpec as P

ALL = ("ctx", "role", "exp")
GROUP = ("role", "exp")
BF16 = jnp.bfloat16
F32 = jnp.float32
SIDE = 4
LANES = 128


def dot(a, b, dims=((1,), (0,))):
    return lax.dot_general(a, b, (dims, ((), ())), preferred_element_type=F32)


def shift_z(block, step):
    return lax.ppermute(block, GROUP, [(g, (g + 2 * step) % 8) for g in range(8)])


def swap_core(block):
    return lax.ppermute(block, GROUP, [(g, g ^ 1) for g in range(8)])


def shift_plane(block, phase, step):
    pairs = []
    for c in range(SIDE * SIDE):
        x, y = divmod(c, SIDE)
        for g in range(8):
            if g % 2 == phase:
                to = x * SIDE + (y + step) % SIDE
            else:
                to = (x + step) % SIDE * SIDE + y
            pairs.append((c * 8 + g, to * 8 + g))
    return lax.ppermute(block, ALL, pairs)


def ring_list(block, shift):
    half = block.shape[0] // 2
    before = shift(block, 1)
    after = shift(block, -1)
    far = [shift(before[:half], 1), shift(after[half:], -1)]
    return [block, after, far, before]


def ctx_gather(block):
    own, after, far, before = ring_list(block, lambda b, s: shift_plane(b, 0, s))
    first = jnp.stack([own, after, jnp.concatenate(far, 0), before])
    own, after, far, before = ring_list(first, lambda b, s: shift_plane(b, 1, s))
    return [own, after, *far, before]


def group_gather(block):
    own, after, far, before = ring_list(block, shift_z)
    rows = [own, after, jnp.concatenate(far, 0), before]
    return [part for own in rows for part in (own, swap_core(own))]


def group_exchange(blocks):
    received = [
        blocks[0],
        shift_z(blocks[3], -1),
        shift_z(blocks[2], 2),
        shift_z(blocks[1], 1),
    ]
    return [part for pair in received for part in (pair, swap_core(pair))]


def roll_lead(array, shift, axis):
    twice = jnp.concatenate([array, array], axis)
    return lax.dynamic_slice_in_dim(twice, shift, SIDE, axis)


def split3(value):
    high = lax.reduce_precision(value, 8, 7)
    rest = value - high
    middle = lax.reduce_precision(rest, 8, 7)
    low = lax.reduce_precision(rest - middle, 8, 7)
    return [term.astype(BF16) for term in (high, middle, low)]


def pad_lanes(terms):
    rows = terms[0].shape[0]
    blank = jnp.zeros((rows, LANES - len(terms)), BF16)
    return jnp.concatenate([t.reshape(rows, 1) for t in terms] + [blank], 1)


def lanes3(value):
    lane = lax.broadcasted_iota(jnp.int32, (value.shape[0], LANES), 1)
    high = value.astype(BF16).astype(F32)
    rest = value - high
    middle = rest.astype(BF16).astype(F32)
    low = rest - middle
    wide = jnp.where(lane == 0, high, jnp.where(lane == 1, middle, jnp.where(lane == 2, low, 0.0)))
    return wide.astype(BF16)


def call(kernel, outs, scalars=0, **params):
    def run(*operands):
        spaces = [pltpu.SMEM] * scalars + [pltpu.VMEM] * (len(operands) - scalars)
        return pl.pallas_call(
            kernel,
            out_shape=outs,
            in_specs=[pl.BlockSpec(memory_space=space) for space in spaces],
            **params,
        )(*operands)

    return run


def member(place_ref, step, other):
    z = lax.rem(place_ref[0] + step, SIDE)
    return 2 * z + place_ref[1] + other - 2 * place_ref[1] * other


def prepare_kernel(place_ref, down_ref, gate_ref, up_ref, *outs):
    slice_width = outs[0].shape[1]
    hidden = down_ref.shape[0]
    for step in range(SIDE):
        for other in range(2):
            start = pl.multiple_of(member(place_ref, step, other) * slice_width, LANES)
            outs[step][other, :, :hidden] = gate_ref[pl.ds(start, slice_width), :]
            outs[step][other, :, hidden : 2 * hidden] = up_ref[pl.ds(start, slice_width), :]
            outs[step][other, :, 2 * hidden :] = down_ref[:, pl.ds(start, slice_width)].T


def attend_kernel(scale, q_ref, near_ref, far_ref, key_frame_ref, own_frame_ref, uv_ref, out_ref):
    heads, latent_width, value_width = uv_ref.shape
    tokens = q_ref.shape[0]
    keys = [near_ref[...], far_ref[...]]
    count = keys[0].shape[0]
    query = jnp.concatenate(
        [q_ref[:, h * latent_width : (h + 1) * latent_width] for h in range(heads)], 0
    )
    own = own_frame_ref[...]
    scores = []
    for part in range(2):
        visible = key_frame_ref[:, part * count : (part + 1) * count] <= own
        visible = jnp.concatenate([visible.astype(F32)] * heads, 0) > 0.5
        scores.append(jnp.where(visible, dot(query, keys[part], ((1,), (1,))) * scale, -1e30))
    top = jnp.maximum(*[jnp.max(s, axis=1, keepdims=True) for s in scores])
    weights = [jnp.exp(s - top) for s in scores]
    total = sum(jnp.sum(w, axis=1, keepdims=True) for w in weights)
    mix = sum(dot(w.astype(BF16), k) for w, k in zip(weights, keys))
    mix = (mix / total).astype(BF16)
    for h in range(heads):
        out_ref[:, h * value_width : (h + 1) * value_width] = dot(
            mix[h * tokens : (h + 1) * tokens], uv_ref[h]
        ).astype(BF16)


def out_proj_kernel(place_ref, *refs):
    piece_refs, weight_refs, out_ref = refs[:5], refs[5:13], refs[13]
    tokens, columns = out_ref.shape[1:]
    depth = weight_refs[0].shape[0]
    total = jnp.zeros((SIDE * SIDE * tokens, columns), F32)
    for block in range(8):
        start = pl.multiple_of(member(place_ref, block // 2, block % 2) * depth, LANES)
        rows = jnp.concatenate(
            [ref[i, :, pl.ds(start, depth)] for ref in piece_refs for i in range(ref.shape[0])], 0
        )
        total = total + dot(rows, weight_refs[block][...])
    total = total.astype(BF16)
    core = place_ref[1]
    for i in range(SIDE):
        for j in range(SIDE):
            step_x = i + core * (j - i)
            step_y = j + core * (i - j)
            owner = lax.rem(place_ref[2] + step_x, SIDE) * SIDE + lax.rem(
                place_ref[3] + step_y, SIDE
            )
            first = (i * SIDE + j) * tokens
            out_ref[owner] = total[first : first + tokens]


def expert_kernel(*refs):
    row_refs, grad_refs, weight_refs, out_ref = refs[:8], refs[8:16], refs[16:20], refs[20]
    hidden = weight_refs[0].shape[2] // 3
    both, hidden_grad = 0.0, 0.0
    for place in range(8):
        weight_ref, other = weight_refs[place // 2], place % 2
        both = both + dot(row_refs[place][...], weight_ref[other, :, : 2 * hidden])
        hidden_grad = hidden_grad + dot(grad_refs[place][...], weight_ref[other, :, 2 * hidden :])
    gate_in, up_in = both[:, :hidden], both[:, hidden:]
    gate_sig = 1.0 / (1.0 + jnp.exp(-gate_in))
    silu = gate_in * gate_sig
    gate_grad = hidden_grad * up_in * gate_sig * (1.0 + gate_in * (1.0 - gate_sig))
    up_grad = hidden_grad * silu
    center = jnp.sum(gate_grad * gate_in + up_grad * up_in, axis=1, keepdims=True)
    out_ref[:, :hidden] = gate_grad.astype(BF16)
    out_ref[:, hidden : 2 * hidden] = up_grad.astype(BF16)
    out_ref[:, 2 * hidden : 3 * hidden] = (silu * up_in).astype(BF16)
    out_ref[:, 3 * hidden :] = lanes3(center)


def weight_grad_kernel(place_ref, *refs):
    row_refs, grad_refs, hidden_ref = refs[:8], refs[8:16], refs[16]
    gate_ref, up_ref, down_ref = refs[17:]
    hidden = gate_ref.shape[1]
    slice_width = row_refs[0].shape[1]
    grads = hidden_ref[:, : 2 * hidden]
    units = hidden_ref[:, 2 * hidden : 3 * hidden]
    for place in range(8):
        start = pl.multiple_of(member(place_ref, place // 2, place % 2) * slice_width, LANES)
        both = dot(row_refs[place][...], grads, ((0,), (0,)))
        gate_ref[pl.ds(start, slice_width), :] = both[:, :hidden].astype(BF16)
        up_ref[pl.ds(start, slice_width), :] = both[:, hidden:].astype(BF16)
        down_ref[:, pl.ds(start, slice_width)] = dot(
            units, grad_refs[place][...], ((0,), (0,))
        ).astype(BF16)


def project_kernel(*refs):
    member_refs, weight_refs, out_ref = refs[:8], refs[8:16], refs[16]
    slice_width, wide = weight_refs[0].shape[1:]
    hidden = wide // 3
    rows, grads, center = 0.0, 0.0, 0.0
    for place in range(8):
        member_ref, weight = member_refs[place], weight_refs[place][place % 2]
        grads = grads + dot(member_ref[:, : 2 * hidden], weight[:, : 2 * hidden], ((1,), (1,)))
        rows = rows + dot(
            member_ref[:, 2 * hidden : 3 * hidden], weight[:, 2 * hidden :], ((1,), (1,))
        )
        center = center + jnp.sum(member_ref[:, 3 * hidden :].astype(F32), axis=1, keepdims=True)
    rows, grads, center = rows.astype(BF16), grads.astype(BF16), lanes3(center)
    sources, capacity = out_ref.shape[:2]
    for source in range(sources):
        part = slice(source * capacity, (source + 1) * capacity)
        out_ref[source, :, :slice_width] = rows[part]
        out_ref[source, :, slice_width : 2 * slice_width] = grads[part]
        out_ref[source, :, 2 * slice_width :] = center[part]


def per_device(
    queries,
    latent,
    frames,
    w_uv,
    w_out,
    residual,
    norm_gain,
    expert_ids,
    mix_codes,
    w_gate,
    w_up,
    w_down,
    grad_out,
):
    ctx_count = lax.axis_size("ctx")
    ctx_place = lax.axis_index("ctx")
    plane_x, plane_y = ctx_place // SIDE, ctx_place % SIDE
    group_place = lax.axis_index(GROUP)
    place_z, core = group_place // 2, group_place % 2
    group_count = 8
    token_count = queries.shape[0]
    head_count, latent_width, value_width = w_uv.shape
    model_width = w_gate.shape[1]
    slice_width = residual.shape[1]
    top_count = expert_ids.shape[1]
    hidden_width = w_gate.shape[2]
    column_width = w_out.shape[1]
    part_tokens = token_count // group_count
    capacity = token_count * top_count // ctx_count * 5 // 4
    slot_total = ctx_count * capacity

    def shape(*dims):
        return jax.ShapeDtypeStruct(dims, BF16)

    places = jnp.stack([place_z, core, plane_x, plane_y]).astype(jnp.int32)

    out_weight = group_gather(w_out)
    weight_blocks = call(
        prepare_kernel, [shape(2, slice_width, 3 * hidden_width)] * SIDE, 1
    )(places, w_down[0], w_gate[0], w_up[0])
    slice_weights = group_exchange(weight_blocks)

    shares = residual.reshape(SIDE, 2, part_tokens, slice_width)
    shares = roll_lead(shares, place_z, 0)
    shares = jnp.where(core == 0, shares, shares[:, ::-1])
    shares = group_exchange([shares[i] for i in range(SIDE)])
    shares = jnp.stack([pair[place % 2] for place, pair in enumerate(shares)])
    shares = shares.reshape(SIDE, 2, part_tokens, slice_width)
    shares = jnp.where(core == 0, shares, shares[:, ::-1])
    shares = roll_lead(shares, (SIDE - place_z) % SIDE, 0)
    residual_part = jnp.transpose(
        shares.reshape(group_count, part_tokens, slice_width), (1, 0, 2)
    ).reshape(part_tokens, model_width)

    chosen = expert_ids.reshape(-1)
    pair_range = jnp.arange(token_count * top_count, dtype=jnp.int32)
    same = (chosen[:, None] == chosen[None, :]) & (pair_range[None, :] < pair_range[:, None])
    earlier = jnp.sum(same.astype(jnp.int32), axis=1)
    slot_index = (chosen * capacity + earlier).reshape(token_count, top_count)
    slot_range = jnp.arange(slot_total, dtype=jnp.int32)
    code_values = mix_codes.astype(F32)
    mix_weight = code_values / jnp.sum(code_values, axis=1, keepdims=True)
    hits = [slot_index[:, k][None, :] == slot_range[:, None] for k in range(top_count)]
    pick = sum(hit.astype(F32) for hit in hits).astype(BF16)
    slot_weight = sum(
        jnp.sum(jnp.where(hits[k], mix_weight[:, k][None, :], 0.0), axis=1) for k in range(top_count)
    )
    returns = [
        (slot_index[:, k][:, None] == slot_range[None, :]).astype(BF16) for k in range(top_count)
    ]

    def to_experts(rows):
        return lax.all_to_all(rows, "ctx", split_axis=0, concat_axis=0, tiled=True)

    grad_rows = (dot(pick, grad_out) * slot_weight[:, None]).astype(BF16)
    grad_rows = to_experts(grad_rows)
    out_grad = group_gather(grad_rows)

    half = token_count // 2
    own_keys = ctx_gather(lax.dynamic_slice_in_dim(latent, core * half, half, 0))
    own_keys = jnp.concatenate(own_keys, 0).reshape(ctx_count * half, latent_width)
    other_keys = swap_core(own_keys)
    own_frames = lax.dynamic_slice_in_dim(frames, ctx_place * token_count, token_count)
    frame_grid = frames.reshape(SIDE, SIDE, 2, half)
    frame_grid = roll_lead(roll_lead(frame_grid, plane_x, 0), plane_y, 1)
    by_x = jnp.transpose(frame_grid, (2, 0, 1, 3))
    by_y = jnp.transpose(frame_grid, (2, 1, 0, 3))
    key_frames = jnp.where(
        core == 0,
        jnp.concatenate([by_x[0].reshape(-1), by_y[1].reshape(-1)]),
        jnp.concatenate([by_y[1].reshape(-1), by_x[0].reshape(-1)]),
    )
    heads = 2
    head_out = pl.pallas_call(
        functools.partial(attend_kernel, latent_width ** (-0.5)),
        out_shape=shape(token_count, head_count * value_width),
        grid=(head_count // heads,),
        in_specs=[
            pl.BlockSpec((token_count, heads * latent_width), lambda h: (0, h)),
            pl.BlockSpec(own_keys.shape, lambda h: (0, 0)),
            pl.BlockSpec(other_keys.shape, lambda h: (0, 0)),
            pl.BlockSpec((1, ctx_count * token_count), lambda h: (0, 0)),
            pl.BlockSpec((token_count, 1), lambda h: (0, 0)),
            pl.BlockSpec((heads, latent_width, value_width), lambda h: (h, 0, 0)),
        ],
        out_specs=pl.BlockSpec((token_count, heads * value_width), lambda h: (0, h)),
        name="attend",
    )(queries, own_keys, other_keys, key_frames[None], own_frames[:, None], w_uv)
    head_out = head_out.reshape(group_count, part_tokens, head_count * value_width)

    head_part = lax.all_to_all(head_out, GROUP, 0, 0, tiled=True)
    head_part = jnp.transpose(head_part, (1, 0, 2)).reshape(part_tokens, -1)
    columns = call(out_proj_kernel, shape(ctx_count, part_tokens, column_width), 1)(
        places, *ctx_gather(head_part), *out_weight
    )
    columns = to_experts(columns)
    attn_part = jnp.transpose(columns, (1, 0, 2)).reshape(part_tokens, model_width)
    pre_part = (residual_part.astype(F32) + attn_part.astype(F32)).astype(BF16)
    pre_wide = pre_part.astype(F32)
    inv_part = lax.rsqrt(jnp.mean(pre_wide * pre_wide, axis=-1, keepdims=True) + 1e-06)
    inv_lanes = pad_lanes(split3(inv_part))
    pre_send = jnp.concatenate(
        [
            jnp.transpose(pre_part.reshape(part_tokens, group_count, slice_width), (1, 0, 2)),
            jnp.broadcast_to(inv_lanes[None], (group_count, part_tokens, 128)),
        ],
        2,
    )
    pre_back = lax.all_to_all(pre_send, GROUP, 0, 0, tiled=True).reshape(token_count, -1)
    pre_norm = pre_back[:, :slice_width].astype(F32)
    inv_scale = jnp.sum(pre_back[:, slice_width : slice_width + 3].astype(F32), axis=1, keepdims=True)
    unit_rows = pre_norm * inv_scale
    local_gain = lax.dynamic_slice_in_dim(norm_gain, group_place * slice_width, slice_width)
    normed = (unit_rows * local_gain).astype(BF16)

    expert_rows = group_gather(to_experts(dot(pick, normed).astype(BF16)))
    hidden_send = call(expert_kernel, shape(slot_total, 3 * hidden_width + LANES))(
        *expert_rows, *out_grad, *weight_blocks
    )
    members = group_gather(hidden_send)
    grad_gate, grad_up, grad_down = call(
        weight_grad_kernel,
        [shape(model_width, hidden_width)] * 2 + [shape(hidden_width, model_width)],
        1,
    )(places, *expert_rows, *out_grad, hidden_send)
    grad_gate, grad_up, grad_down = grad_gate[None], grad_up[None], grad_down[None]
    back = call(
        project_kernel, shape(ctx_count, capacity, 2 * slice_width + LANES)
    )(*members, *slice_weights)
    back = to_experts(back).reshape(slot_total, 2 * slice_width + LANES)

    routed = sum(
        dot(returns[k], back[:, :slice_width]) * mix_weight[:, k : k + 1] for k in range(top_count)
    )
    layer_out = (pre_norm + routed).astype(BF16)
    summed = dot(returns[0] + returns[1], back[:, slice_width:])
    normed_grad = summed[:, :slice_width].astype(BF16).astype(F32)
    center = jnp.sum(summed[:, slice_width : slice_width + 3], axis=1, keepdims=True) / model_width
    scaled_grad = normed_grad * local_gain
    grad_pre_norm = (
        grad_out.astype(F32) + inv_scale * (scaled_grad - unit_rows * center)
    ).astype(BF16)
    return (layer_out, grad_pre_norm, grad_gate, grad_up, grad_down)


def solution(mesh):
    placed = (
        P("ctx", ("role", "exp")),
        P("ctx", None),
        P(),
        P(("role", "exp"), None, None),
        P(("role", "exp"), "ctx"),
        P("ctx", ("role", "exp")),
        P(),
        P("ctx", None),
        P("ctx", None),
        P("ctx", None, ("role", "exp")),
        P("ctx", None, ("role", "exp")),
        P("ctx", ("role", "exp"), None),
        P("ctx", ("role", "exp")),
    )

    return jax.shard_map(
        per_device,
        mesh=mesh,
        in_specs=placed,
        out_specs=(
            P("ctx", ("role", "exp")),
            P("ctx", ("role", "exp")),
            P("ctx", None, ("role", "exp")),
            P("ctx", None, ("role", "exp")),
            P("ctx", ("role", "exp"), None),
        ),
        check_vma=False,
    )
```

```python
import functools

import jax
import jax.numpy as jnp
from jax import lax
from jax.experimental import pallas as pl
from jax.experimental.pallas import tpu as pltpu
from jax.sharding import PartitionSpec as P

ALL = ("ctx", "role", "exp")
GROUP = ("role", "exp")
BF16 = jnp.bfloat16
F32 = jnp.float32
SIDE = 4
LANES = 128


def dot(a, b, dims=((1,), (0,))):
    return lax.dot_general(a, b, (dims, ((), ())), preferred_element_type=F32)


def shift_z(block, step):
    return lax.ppermute(block, GROUP, [(g, (g + 2 * step) % 8) for g in range(8)])


def swap_core(block):
    return lax.ppermute(block, GROUP, [(g, g ^ 1) for g in range(8)])


def shift_plane(block, phase, step):
    pairs = []
    for c in range(SIDE * SIDE):
        x, y = divmod(c, SIDE)
        for g in range(8):
            if g % 2 == phase:
                to = x * SIDE + (y + step) % SIDE
            else:
                to = (x + step) % SIDE * SIDE + y
            pairs.append((c * 8 + g, to * 8 + g))
    return lax.ppermute(block, ALL, pairs)


def ring_list(block, shift):
    half = block.shape[0] // 2
    before = shift(block, 1)
    after = shift(block, -1)
    far = [shift(before[:half], 1), shift(after[half:], -1)]
    return [block, after, far, before]


def ctx_gather(block):
    own, after, far, before = ring_list(block, lambda b, s: shift_plane(b, 0, s))
    first = jnp.stack([own, after, jnp.concatenate(far, 0), before])
    own, after, far, before = ring_list(first, lambda b, s: shift_plane(b, 1, s))
    return [own, after, *far, before]


def group_gather(block):
    return lax.all_gather(block, GROUP, axis=0)


def group_exchange(blocks):
    received = [
        blocks[0],
        shift_z(blocks[3], -1),
        shift_z(blocks[2], 2),
        shift_z(blocks[1], 1),
    ]
    return [part for pair in received for part in (pair, swap_core(pair))]


def roll_lead(array, shift, axis):
    twice = jnp.concatenate([array, array], axis)
    return lax.dynamic_slice_in_dim(twice, shift, SIDE, axis)


def split3(value):
    high = lax.reduce_precision(value, 8, 7)
    rest = value - high
    middle = lax.reduce_precision(rest, 8, 7)
    low = lax.reduce_precision(rest - middle, 8, 7)
    return [term.astype(BF16) for term in (high, middle, low)]


def pad_lanes(terms):
    rows = terms[0].shape[0]
    blank = jnp.zeros((rows, LANES - len(terms)), BF16)
    return jnp.concatenate([t.reshape(rows, 1) for t in terms] + [blank], 1)


def lanes3(value):
    lane = lax.broadcasted_iota(jnp.int32, (value.shape[0], LANES), 1)
    high = value.astype(BF16).astype(F32)
    rest = value - high
    middle = rest.astype(BF16).astype(F32)
    low = rest - middle
    wide = jnp.where(lane == 0, high, jnp.where(lane == 1, middle, jnp.where(lane == 2, low, 0.0)))
    return wide.astype(BF16)


def call(kernel, outs, scalars=0, unread=0, **params):
    def run(*operands):
        whole = len(operands) - scalars - unread
        spaces = [pltpu.SMEM] * scalars + [pltpu.VMEM] * whole + [pl.ANY] * unread
        return pl.pallas_call(
            kernel,
            out_shape=outs,
            in_specs=[pl.BlockSpec(memory_space=space) for space in spaces],
            **params,
        )(*operands)

    return run


def member(place_ref, step, other):
    z = lax.rem(place_ref[0] + step, SIDE)
    return 2 * z + place_ref[1] + other - 2 * place_ref[1] * other


def prepare_kernel(place_ref, down_ref, gate_ref, up_ref, *outs):
    slice_width = outs[0].shape[1]
    hidden = down_ref.shape[0]
    for step in range(SIDE):
        for other in range(2):
            start = pl.multiple_of(member(place_ref, step, other) * slice_width, LANES)
            outs[step][other, :, :hidden] = gate_ref[pl.ds(start, slice_width), :]
            outs[step][other, :, hidden : 2 * hidden] = up_ref[pl.ds(start, slice_width), :]
            outs[step][other, :, 2 * hidden :] = down_ref[:, pl.ds(start, slice_width)].T


def attend_kernel(scale, q_ref, near_ref, far_ref, key_frame_ref, own_frame_ref, uv_ref, out_ref):
    heads, latent_width, value_width = uv_ref.shape
    tokens = q_ref.shape[0]
    keys = [near_ref[...], far_ref[...]]
    count = keys[0].shape[0]
    query = jnp.concatenate(
        [q_ref[:, h * latent_width : (h + 1) * latent_width] for h in range(heads)], 0
    )
    own = own_frame_ref[...]
    scores = []
    for part in range(2):
        visible = key_frame_ref[:, part * count : (part + 1) * count] <= own
        visible = jnp.concatenate([visible.astype(F32)] * heads, 0) > 0.5
        scores.append(jnp.where(visible, dot(query, keys[part], ((1,), (1,))) * scale, -1e30))
    top = jnp.maximum(*[jnp.max(s, axis=1, keepdims=True) for s in scores])
    weights = [jnp.exp(s - top) for s in scores]
    total = sum(jnp.sum(w, axis=1, keepdims=True) for w in weights)
    mix = sum(dot(w.astype(BF16), k) for w, k in zip(weights, keys))
    mix = (mix / total).astype(BF16)
    for h in range(heads):
        out_ref[:, h * value_width : (h + 1) * value_width] = dot(
            mix[h * tokens : (h + 1) * tokens], uv_ref[h]
        ).astype(BF16)


def out_proj_kernel(rows_ref, weight_ref, *refs):
    out_ref = refs[-1]
    members, columns, depth = weight_ref.shape
    total = jnp.zeros((rows_ref.shape[0] * rows_ref.shape[1], columns), F32)
    for place in range(members):
        rows = rows_ref[:, :, place * depth : (place + 1) * depth]
        rows = rows.reshape(total.shape[0], depth)
        total = total + dot(rows, weight_ref[place], ((1,), (1,)))
    out_ref[...] = total.astype(BF16).reshape(out_ref.shape)


def expert_kernel(place_ref, rows_ref, grads_ref, *refs):
    weight_refs, out_ref = refs[:4], refs[4]
    hidden = weight_refs[0].shape[2] // 3
    both, hidden_grad = 0.0, 0.0
    for place in range(8):
        weight_ref, other = weight_refs[place // 2], place % 2
        source = member(place_ref, place // 2, other)
        both = both + dot(rows_ref[source], weight_ref[other, :, : 2 * hidden])
        hidden_grad = hidden_grad + dot(grads_ref[source], weight_ref[other, :, 2 * hidden :])
    gate_in, up_in = both[:, :hidden], both[:, hidden:]
    gate_sig = 1.0 / (1.0 + jnp.exp(-gate_in))
    silu = gate_in * gate_sig
    gate_grad = hidden_grad * up_in * gate_sig * (1.0 + gate_in * (1.0 - gate_sig))
    up_grad = hidden_grad * silu
    center = jnp.sum(gate_grad * gate_in + up_grad * up_in, axis=1, keepdims=True)
    out_ref[:, :hidden] = gate_grad.astype(BF16)
    out_ref[:, hidden : 2 * hidden] = up_grad.astype(BF16)
    out_ref[:, 2 * hidden : 3 * hidden] = (silu * up_in).astype(BF16)
    out_ref[:, 3 * hidden :] = lanes3(center)


def weight_grad_kernel(rows_ref, grads_ref, hidden_ref, gate_ref, up_ref, down_ref):
    hidden = gate_ref.shape[1]
    members, _, slice_width = rows_ref.shape
    grads = hidden_ref[:, : 2 * hidden]
    units = hidden_ref[:, 2 * hidden : 3 * hidden]
    for place in range(members):
        part = slice(place * slice_width, (place + 1) * slice_width)
        both = dot(rows_ref[place], grads, ((0,), (0,)))
        gate_ref[part, :] = both[:, :hidden].astype(BF16)
        up_ref[part, :] = both[:, hidden:].astype(BF16)
        down_ref[:, part] = dot(units, grads_ref[place], ((0,), (0,))).astype(BF16)


def project_kernel(place_ref, hidden_ref, *refs):
    weight_refs, out_ref = refs[:8], refs[8]
    slice_width, wide = weight_refs[0].shape[1:]
    hidden = wide // 3
    rows, grads, center = 0.0, 0.0, 0.0
    for place in range(8):
        source = member(place_ref, place // 2, place % 2)
        weight = weight_refs[place][place % 2]
        units = hidden_ref[source]
        grads = grads + dot(units[:, : 2 * hidden], weight[:, : 2 * hidden], ((1,), (1,)))
        rows = rows + dot(units[:, 2 * hidden : 3 * hidden], weight[:, 2 * hidden :], ((1,), (1,)))
        center = center + jnp.sum(units[:, 3 * hidden :].astype(F32), axis=1, keepdims=True)
    rows, grads, center = rows.astype(BF16), grads.astype(BF16), lanes3(center)
    sources, capacity = out_ref.shape[:2]
    for source in range(sources):
        part = slice(source * capacity, (source + 1) * capacity)
        out_ref[source, :, :slice_width] = rows[part]
        out_ref[source, :, slice_width : 2 * slice_width] = grads[part]
        out_ref[source, :, 2 * slice_width :] = center[part]


def per_device(
    queries,
    latent,
    frames,
    w_uv,
    w_out,
    residual,
    norm_gain,
    expert_ids,
    mix_codes,
    w_gate,
    w_up,
    w_down,
    grad_out,
):
    ctx_count = lax.axis_size("ctx")
    ctx_place = lax.axis_index("ctx")
    plane_x, plane_y = ctx_place // SIDE, ctx_place % SIDE
    group_place = lax.axis_index(GROUP)
    place_z, core = group_place // 2, group_place % 2
    group_count = 8
    token_count = queries.shape[0]
    head_count, latent_width, value_width = w_uv.shape
    model_width = w_gate.shape[1]
    slice_width = residual.shape[1]
    top_count = expert_ids.shape[1]
    hidden_width = w_gate.shape[2]
    column_width = w_out.shape[1]
    part_tokens = token_count // group_count
    capacity = token_count * top_count // ctx_count * 5 // 4
    slot_total = ctx_count * capacity

    def shape(*dims):
        return jax.ShapeDtypeStruct(dims, BF16)

    places = jnp.stack([place_z, core]).astype(jnp.int32)

    out_weight = group_gather(w_out.T)
    weight_blocks = call(
        prepare_kernel, [shape(2, slice_width, 3 * hidden_width)] * SIDE, 1
    )(places, w_down[0], w_gate[0], w_up[0])
    slice_weights = group_exchange(weight_blocks)

    residual_part = lax.all_to_all(
        residual.reshape(group_count, part_tokens, slice_width), GROUP, 0, 0, tiled=True
    )

    chosen = expert_ids.reshape(-1)
    pair_range = jnp.arange(token_count * top_count, dtype=jnp.int32)
    same = (chosen[:, None] == chosen[None, :]) & (pair_range[None, :] < pair_range[:, None])
    earlier = jnp.sum(same.astype(jnp.int32), axis=1)
    slot_index = (chosen * capacity + earlier).reshape(token_count, top_count)
    slot_range = jnp.arange(slot_total, dtype=jnp.int32)
    code_values = mix_codes.astype(F32)
    mix_weight = code_values / jnp.sum(code_values, axis=1, keepdims=True)
    hits = [slot_index[:, k][None, :] == slot_range[:, None] for k in range(top_count)]
    pick = sum(hit.astype(F32) for hit in hits).astype(BF16)
    slot_weight = sum(
        jnp.sum(jnp.where(hits[k], mix_weight[:, k][None, :], 0.0), axis=1) for k in range(top_count)
    )
    returns = [
        (slot_index[:, k][:, None] == slot_range[None, :]).astype(BF16) for k in range(top_count)
    ]

    def to_experts(rows):
        return lax.all_to_all(rows, "ctx", split_axis=0, concat_axis=0, tiled=True)

    grad_rows = (dot(pick, grad_out) * slot_weight[:, None]).astype(BF16)
    grad_rows = to_experts(grad_rows)
    out_grad = group_gather(grad_rows)

    half = token_count // 2
    own_keys = ctx_gather(lax.dynamic_slice_in_dim(latent, core * half, half, 0))
    own_keys = jnp.concatenate(own_keys, 0).reshape(ctx_count * half, latent_width)
    other_keys = swap_core(own_keys)
    own_frames = lax.dynamic_slice_in_dim(frames, ctx_place * token_count, token_count)
    frame_grid = frames.reshape(SIDE, SIDE, 2, half)
    frame_grid = roll_lead(roll_lead(frame_grid, plane_x, 0), plane_y, 1)
    by_x = jnp.transpose(frame_grid, (2, 0, 1, 3))
    by_y = jnp.transpose(frame_grid, (2, 1, 0, 3))
    key_frames = jnp.where(
        core == 0,
        jnp.concatenate([by_x[0].reshape(-1), by_y[1].reshape(-1)]),
        jnp.concatenate([by_y[1].reshape(-1), by_x[0].reshape(-1)]),
    )
    heads = 2
    head_out = pl.pallas_call(
        functools.partial(attend_kernel, latent_width ** (-0.5)),
        out_shape=shape(token_count, head_count * value_width),
        grid=(head_count // heads,),
        in_specs=[
            pl.BlockSpec((token_count, heads * latent_width), lambda h: (0, h)),
            pl.BlockSpec(own_keys.shape, lambda h: (0, 0)),
            pl.BlockSpec(other_keys.shape, lambda h: (0, 0)),
            pl.BlockSpec((1, ctx_count * token_count), lambda h: (0, 0)),
            pl.BlockSpec((token_count, 1), lambda h: (0, 0)),
            pl.BlockSpec((heads, latent_width, value_width), lambda h: (h, 0, 0)),
        ],
        out_specs=pl.BlockSpec((token_count, heads * value_width), lambda h: (0, h)),
        name="attend",
    )(queries, own_keys, other_keys, key_frames[None], own_frames[:, None], w_uv)
    head_out = head_out.reshape(group_count, part_tokens, head_count * value_width)

    head_part = lax.all_to_all(head_out, GROUP, 0, 0, tiled=True)
    head_part = jnp.transpose(head_part, (1, 0, 2)).reshape(part_tokens, -1)
    all_heads = lax.all_gather(head_part, "ctx", axis=0)
    columns = call(
        out_proj_kernel, shape(ctx_count, part_tokens, column_width), unread=2 + SIDE
    )(all_heads, out_weight, residual_part, grad_rows, *weight_blocks)
    residual_part = jnp.transpose(residual_part, (1, 0, 2)).reshape(part_tokens, model_width)
    columns = to_experts(columns)
    attn_part = jnp.transpose(columns, (1, 0, 2)).reshape(part_tokens, model_width)
    pre_part = (residual_part.astype(F32) + attn_part.astype(F32)).astype(BF16)
    pre_wide = pre_part.astype(F32)
    inv_part = lax.rsqrt(jnp.mean(pre_wide * pre_wide, axis=-1, keepdims=True) + 1e-06)
    inv_lanes = pad_lanes(split3(inv_part))
    pre_send = jnp.concatenate(
        [
            jnp.transpose(pre_part.reshape(part_tokens, group_count, slice_width), (1, 0, 2)),
            jnp.broadcast_to(inv_lanes[None], (group_count, part_tokens, 128)),
        ],
        2,
    )
    pre_back = lax.all_to_all(pre_send, GROUP, 0, 0, tiled=True).reshape(token_count, -1)
    pre_norm = pre_back[:, :slice_width].astype(F32)
    inv_scale = jnp.sum(pre_back[:, slice_width : slice_width + 3].astype(F32), axis=1, keepdims=True)
    unit_rows = pre_norm * inv_scale
    local_gain = lax.dynamic_slice_in_dim(norm_gain, group_place * slice_width, slice_width)
    normed = (unit_rows * local_gain).astype(BF16)

    expert_rows = group_gather(to_experts(dot(pick, normed).astype(BF16)))
    hidden_send = call(expert_kernel, shape(slot_total, 3 * hidden_width + LANES), 1)(
        places, expert_rows, out_grad, *weight_blocks
    )
    hidden_all = group_gather(hidden_send)
    grad_gate, grad_up, grad_down = call(
        weight_grad_kernel,
        [shape(model_width, hidden_width)] * 2 + [shape(hidden_width, model_width)],
    )(expert_rows, out_grad, hidden_send)
    grad_gate, grad_up, grad_down = grad_gate[None], grad_up[None], grad_down[None]
    back = call(
        project_kernel, shape(ctx_count, capacity, 2 * slice_width + LANES), 1
    )(places, hidden_all, *slice_weights)
    back = to_experts(back).reshape(slot_total, 2 * slice_width + LANES)

    routed = sum(
        dot(returns[k], back[:, :slice_width]) * mix_weight[:, k : k + 1] for k in range(top_count)
    )
    layer_out = (pre_norm + routed).astype(BF16)
    summed = dot(returns[0] + returns[1], back[:, slice_width:])
    normed_grad = summed[:, :slice_width].astype(BF16).astype(F32)
    center = jnp.sum(summed[:, slice_width : slice_width + 3], axis=1, keepdims=True) / model_width
    scaled_grad = normed_grad * local_gain
    grad_pre_norm = (
        grad_out.astype(F32) + inv_scale * (scaled_grad - unit_rows * center)
    ).astype(BF16)
    return (layer_out, grad_pre_norm, grad_gate, grad_up, grad_down)


def solution(mesh):
    placed = (
        P("ctx", ("role", "exp")),
        P("ctx", None),
        P(),
        P(("role", "exp"), None, None),
        P(("role", "exp"), "ctx"),
        P("ctx", ("role", "exp")),
        P(),
        P("ctx", None),
        P("ctx", None),
        P("ctx", None, ("role", "exp")),
        P("ctx", None, ("role", "exp")),
        P("ctx", ("role", "exp"), None),
        P("ctx", ("role", "exp")),
    )

    return jax.shard_map(
        per_device,
        mesh=mesh,
        in_specs=placed,
        out_specs=(
            P("ctx", ("role", "exp")),
            P("ctx", ("role", "exp")),
            P("ctx", None, ("role", "exp")),
            P("ctx", None, ("role", "exp")),
            P("ctx", ("role", "exp"), None),
        ),
        check_vma=False,
    )
```

```python
import functools

import jax
import jax.numpy as jnp
from jax import lax
from jax.experimental import pallas as pl
from jax.experimental.pallas import tpu as pltpu
from jax.sharding import PartitionSpec as P

ALL = ("ctx", "role", "exp")
GROUP = ("role", "exp")
BF16 = jnp.bfloat16
F32 = jnp.float32
SIDE = 4
LANES = 128


def dot(a, b, dims=((1,), (0,))):
    return lax.dot_general(a, b, (dims, ((), ())), preferred_element_type=F32)


def shift_z(block, step):
    return lax.ppermute(block, GROUP, [(g, (g + 2 * step) % 8) for g in range(8)])


def swap_core(block):
    return lax.ppermute(block, GROUP, [(g, g ^ 1) for g in range(8)])


def shift_plane(block, phase, step):
    pairs = []
    for c in range(SIDE * SIDE):
        x, y = divmod(c, SIDE)
        for g in range(8):
            if g % 2 == phase:
                to = x * SIDE + (y + step) % SIDE
            else:
                to = (x + step) % SIDE * SIDE + y
            pairs.append((c * 8 + g, to * 8 + g))
    return lax.ppermute(block, ALL, pairs)


def ring_list(block, shift):
    half = block.shape[0] // 2
    before = shift(block, 1)
    after = shift(block, -1)
    far = [shift(before[:half], 1), shift(after[half:], -1)]
    return [block, after, far, before]


def ctx_gather(block):
    own, after, far, before = ring_list(block, lambda b, s: shift_plane(b, 0, s))
    first = jnp.stack([own, after, jnp.concatenate(far, 0), before])
    own, after, far, before = ring_list(first, lambda b, s: shift_plane(b, 1, s))
    return [own, after, *far, before]


def group_gather(block):
    return lax.all_gather(block, GROUP, axis=0)


def group_exchange(blocks):
    received = [
        blocks[0],
        shift_z(blocks[3], -1),
        shift_z(blocks[2], 2),
        shift_z(blocks[1], 1),
    ]
    return [part for pair in received for part in (pair, swap_core(pair))]


def roll_lead(array, shift, axis):
    twice = jnp.concatenate([array, array], axis)
    return lax.dynamic_slice_in_dim(twice, shift, SIDE, axis)


def split3(value):
    high = lax.reduce_precision(value, 8, 7)
    rest = value - high
    middle = lax.reduce_precision(rest, 8, 7)
    low = lax.reduce_precision(rest - middle, 8, 7)
    return [term.astype(BF16) for term in (high, middle, low)]


def pad_lanes(terms):
    rows = terms[0].shape[0]
    blank = jnp.zeros((rows, LANES - len(terms)), BF16)
    return jnp.concatenate([t.reshape(rows, 1) for t in terms] + [blank], 1)


def lanes3(value):
    lane = lax.broadcasted_iota(jnp.int32, (value.shape[0], LANES), 1)
    high = value.astype(BF16).astype(F32)
    rest = value - high
    middle = rest.astype(BF16).astype(F32)
    low = rest - middle
    wide = jnp.where(lane == 0, high, jnp.where(lane == 1, middle, jnp.where(lane == 2, low, 0.0)))
    return wide.astype(BF16)


def call(kernel, outs, scalars=0, whole=None, **params):
    def run(*operands):
        count = len(operands) - scalars if whole is None else whole
        left = len(operands) - scalars - count
        spaces = [pltpu.SMEM] * scalars + [pltpu.VMEM] * count + [pl.ANY] * left
        return pl.pallas_call(
            kernel,
            out_shape=outs,
            in_specs=[pl.BlockSpec(memory_space=space) for space in spaces],
            **params,
        )(*operands)

    return run


def buffers(*shapes):
    return [pltpu.VMEM(shape, BF16) for shape in shapes] + [
        pltpu.SemaphoreType.DMA((len(shapes), shapes[0][0]))
    ]


def start_copies(lists, bufs, sems):
    copies = [
        [
            pltpu.make_async_copy(source, buf.at[place], sems.at[n, place])
            for place, source in enumerate(sources)
        ]
        for n, (sources, buf) in enumerate(zip(lists, bufs))
    ]
    for group in zip(*copies):
        for copy in group:
            copy.start()
    return copies


def member(place_ref, step, other):
    z = lax.rem(place_ref[0] + step, SIDE)
    return 2 * z + place_ref[1] + other - 2 * place_ref[1] * other


def prepare_kernel(place_ref, down_ref, gate_ref, up_ref, all_ref, *outs):
    slice_width = all_ref.shape[1]
    hidden = down_ref.shape[0]
    for place in range(8):
        step, other = place // 2, place % 2
        start = pl.multiple_of(member(place_ref, step, other) * slice_width, LANES)
        gate = gate_ref[pl.ds(start, slice_width), :]
        up = up_ref[pl.ds(start, slice_width), :]
        down = down_ref[:, pl.ds(start, slice_width)].T
        for at, ref in ((place, all_ref), (other, outs[step])):
            ref[at, :, :hidden] = gate
            ref[at, :, hidden : 2 * hidden] = up
            ref[at, :, 2 * hidden :] = down


def attend_kernel(scale, q_ref, near_ref, far_ref, key_frame_ref, own_frame_ref, uv_ref, out_ref):
    heads, latent_width, value_width = uv_ref.shape
    tokens = q_ref.shape[0]
    keys = [near_ref[...], far_ref[...]]
    count = keys[0].shape[0]
    query = jnp.concatenate(
        [q_ref[:, h * latent_width : (h + 1) * latent_width] for h in range(heads)], 0
    )
    own = own_frame_ref[...]
    scores = []
    for part in range(2):
        visible = key_frame_ref[:, part * count : (part + 1) * count] <= own
        visible = jnp.concatenate([visible.astype(F32)] * heads, 0) > 0.5
        scores.append(jnp.where(visible, dot(query, keys[part], ((1,), (1,))) * scale, -1e30))
    top = jnp.maximum(*[jnp.max(s, axis=1, keepdims=True) for s in scores])
    weights = [jnp.exp(s - top) for s in scores]
    total = sum(jnp.sum(w, axis=1, keepdims=True) for w in weights)
    mix = sum(dot(w.astype(BF16), k) for w, k in zip(weights, keys))
    mix = (mix / total).astype(BF16)
    for h in range(heads):
        out_ref[:, h * value_width : (h + 1) * value_width] = dot(
            mix[h * tokens : (h + 1) * tokens], uv_ref[h]
        ).astype(BF16)


def out_proj_kernel(rows_ref, weight_ref, *refs):
    out_ref, row_buf, weight_buf, sems = refs[-4:]
    members, columns, depth = weight_ref.shape
    copies = start_copies(
        [
            [rows_ref.at[:, :, pl.ds(p * depth, depth)] for p in range(members)],
            [weight_ref.at[p] for p in range(members)],
        ],
        [row_buf, weight_buf],
        sems,
    )
    total = jnp.zeros((rows_ref.shape[0] * rows_ref.shape[1], columns), F32)
    for place in range(members):
        for copy in copies:
            copy[place].wait()
        rows = row_buf[place].reshape(total.shape[0], depth)
        total = total + dot(rows, weight_buf[place], ((1,), (1,)))
    out_ref[...] = total.astype(BF16).reshape(out_ref.shape)


def expert_kernel(place_ref, rows_ref, grads_ref, weight_ref, out_ref, *scratch):
    row_buf, grad_buf, weight_buf, sems = scratch
    sources = [member(place_ref, p // 2, p % 2) for p in range(8)]
    copies = start_copies(
        [
            [grads_ref.at[source] for source in sources],
            [rows_ref.at[source] for source in sources],
            [weight_ref.at[p] for p in range(8)],
        ],
        [grad_buf, row_buf, weight_buf],
        sems,
    )
    hidden = weight_ref.shape[2] // 3
    both, hidden_grad = 0.0, 0.0
    for place in range(8):
        for copy in copies:
            copy[place].wait()
        both = both + dot(row_buf[place], weight_buf[place, :, : 2 * hidden])
        hidden_grad = hidden_grad + dot(grad_buf[place], weight_buf[place, :, 2 * hidden :])
    gate_in, up_in = both[:, :hidden], both[:, hidden:]
    gate_sig = 1.0 / (1.0 + jnp.exp(-gate_in))
    silu = gate_in * gate_sig
    gate_grad = hidden_grad * up_in * gate_sig * (1.0 + gate_in * (1.0 - gate_sig))
    up_grad = hidden_grad * silu
    center = jnp.sum(gate_grad * gate_in + up_grad * up_in, axis=1, keepdims=True)
    out_ref[:, :hidden] = gate_grad.astype(BF16)
    out_ref[:, hidden : 2 * hidden] = up_grad.astype(BF16)
    out_ref[:, 2 * hidden : 3 * hidden] = (silu * up_in).astype(BF16)
    out_ref[:, 3 * hidden :] = lanes3(center)


def weight_grad_kernel(rows_ref, grads_ref, hidden_ref, gate_ref, up_ref, down_ref):
    hidden = gate_ref.shape[1]
    members, _, slice_width = rows_ref.shape
    grads = hidden_ref[:, : 2 * hidden]
    units = hidden_ref[:, 2 * hidden : 3 * hidden]
    for place in range(members):
        part = slice(place * slice_width, (place + 1) * slice_width)
        both = dot(rows_ref[place], grads, ((0,), (0,)))
        gate_ref[part, :] = both[:, :hidden].astype(BF16)
        up_ref[part, :] = both[:, hidden:].astype(BF16)
        down_ref[:, part] = dot(units, grads_ref[place], ((0,), (0,))).astype(BF16)


def project_kernel(place_ref, hidden_ref, *refs):
    weight_refs, out_ref, unit_buf, weight_buf, sems = refs[:8], *refs[8:]
    copies = start_copies(
        [
            [hidden_ref.at[member(place_ref, p // 2, p % 2)] for p in range(8)],
            [weight_refs[p].at[p % 2] for p in range(8)],
        ],
        [unit_buf, weight_buf],
        sems,
    )
    slice_width, wide = weight_refs[0].shape[1:]
    hidden = wide // 3
    rows, grads, center = 0.0, 0.0, 0.0
    for place in range(8):
        for copy in copies:
            copy[place].wait()
        units = unit_buf[place]
        weight = weight_buf[place]
        grads = grads + dot(units[:, : 2 * hidden], weight[:, : 2 * hidden], ((1,), (1,)))
        rows = rows + dot(units[:, 2 * hidden : 3 * hidden], weight[:, 2 * hidden :], ((1,), (1,)))
        center = center + jnp.sum(units[:, 3 * hidden :].astype(F32), axis=1, keepdims=True)
    rows, grads, center = rows.astype(BF16), grads.astype(BF16), lanes3(center)
    sources, capacity = out_ref.shape[:2]
    for source in range(sources):
        part = slice(source * capacity, (source + 1) * capacity)
        out_ref[source, :, :slice_width] = rows[part]
        out_ref[source, :, slice_width : 2 * slice_width] = grads[part]
        out_ref[source, :, 2 * slice_width :] = center[part]


def per_device(
    queries,
    latent,
    frames,
    w_uv,
    w_out,
    residual,
    norm_gain,
    expert_ids,
    mix_codes,
    w_gate,
    w_up,
    w_down,
    grad_out,
):
    ctx_count = lax.axis_size("ctx")
    ctx_place = lax.axis_index("ctx")
    plane_x, plane_y = ctx_place // SIDE, ctx_place % SIDE
    group_place = lax.axis_index(GROUP)
    place_z, core = group_place // 2, group_place % 2
    group_count = 8
    token_count = queries.shape[0]
    head_count, latent_width, value_width = w_uv.shape
    model_width = w_gate.shape[1]
    slice_width = residual.shape[1]
    top_count = expert_ids.shape[1]
    hidden_width = w_gate.shape[2]
    column_width = w_out.shape[1]
    part_tokens = token_count // group_count
    capacity = token_count * top_count // ctx_count * 5 // 4
    slot_total = ctx_count * capacity

    def shape(*dims):
        return jax.ShapeDtypeStruct(dims, BF16)

    places = jnp.stack([place_z, core]).astype(jnp.int32)

    out_weight = group_gather(w_out.T)
    block = (slice_width, 3 * hidden_width)
    weight_blocks, *weight_pairs = call(
        prepare_kernel, [shape(8, *block)] + [shape(2, *block)] * SIDE, 1
    )(places, w_down[0], w_gate[0], w_up[0])

    residual_part = lax.all_to_all(
        residual.reshape(group_count, part_tokens, slice_width), GROUP, 0, 0, tiled=True
    )

    chosen = expert_ids.reshape(-1)
    pair_range = jnp.arange(token_count * top_count, dtype=jnp.int32)
    same = (chosen[:, None] == chosen[None, :]) & (pair_range[None, :] < pair_range[:, None])
    earlier = jnp.sum(same.astype(jnp.int32), axis=1)
    slot_index = (chosen * capacity + earlier).reshape(token_count, top_count)
    slot_range = jnp.arange(slot_total, dtype=jnp.int32)
    code_values = mix_codes.astype(F32)
    mix_weight = code_values / jnp.sum(code_values, axis=1, keepdims=True)
    hits = [slot_index[:, k][None, :] == slot_range[:, None] for k in range(top_count)]
    pick = sum(hit.astype(F32) for hit in hits).astype(BF16)
    slot_weight = sum(
        jnp.sum(jnp.where(hits[k], mix_weight[:, k][None, :], 0.0), axis=1) for k in range(top_count)
    )
    returns = [
        (slot_index[:, k][:, None] == slot_range[None, :]).astype(BF16) for k in range(top_count)
    ]

    def to_experts(rows):
        return lax.all_to_all(rows, "ctx", split_axis=0, concat_axis=0, tiled=True)

    grad_rows = (dot(pick, grad_out) * slot_weight[:, None]).astype(BF16)
    grad_rows, *weight_pairs = lax.optimization_barrier((grad_rows, *weight_pairs))
    grad_rows = to_experts(grad_rows)
    out_grad = group_gather(grad_rows)
    slice_weights = group_exchange(weight_pairs)

    half = token_count // 2
    own_keys = ctx_gather(lax.dynamic_slice_in_dim(latent, core * half, half, 0))
    own_keys = jnp.concatenate(own_keys, 0).reshape(ctx_count * half, latent_width)
    other_keys = swap_core(own_keys)
    own_frames = lax.dynamic_slice_in_dim(frames, ctx_place * token_count, token_count)
    frame_grid = frames.reshape(SIDE, SIDE, 2, half)
    frame_grid = roll_lead(roll_lead(frame_grid, plane_x, 0), plane_y, 1)
    by_x = jnp.transpose(frame_grid, (2, 0, 1, 3))
    by_y = jnp.transpose(frame_grid, (2, 1, 0, 3))
    key_frames = jnp.where(
        core == 0,
        jnp.concatenate([by_x[0].reshape(-1), by_y[1].reshape(-1)]),
        jnp.concatenate([by_y[1].reshape(-1), by_x[0].reshape(-1)]),
    )
    heads = 2
    head_out = pl.pallas_call(
        functools.partial(attend_kernel, latent_width ** (-0.5)),
        out_shape=shape(token_count, head_count * value_width),
        grid=(head_count // heads,),
        in_specs=[
            pl.BlockSpec((token_count, heads * latent_width), lambda h: (0, h)),
            pl.BlockSpec(own_keys.shape, lambda h: (0, 0)),
            pl.BlockSpec(other_keys.shape, lambda h: (0, 0)),
            pl.BlockSpec((1, ctx_count * token_count), lambda h: (0, 0)),
            pl.BlockSpec((token_count, 1), lambda h: (0, 0)),
            pl.BlockSpec((heads, latent_width, value_width), lambda h: (h, 0, 0)),
        ],
        out_specs=pl.BlockSpec((token_count, heads * value_width), lambda h: (0, h)),
        name="attend",
    )(queries, own_keys, other_keys, key_frames[None], own_frames[:, None], w_uv)
    head_out = head_out.reshape(group_count, part_tokens, head_count * value_width)

    head_part = lax.all_to_all(head_out, GROUP, 0, 0, tiled=True)
    head_part = jnp.transpose(head_part, (1, 0, 2)).reshape(part_tokens, -1)
    all_heads = lax.all_gather(head_part, "ctx", axis=0)
    columns = call(
        out_proj_kernel,
        shape(ctx_count, part_tokens, column_width),
        whole=0,
        scratch_shapes=buffers(
            (group_count, ctx_count, part_tokens, head_count * value_width),
            (group_count, column_width, head_count * value_width),
        ),
    )(all_heads, out_weight, residual_part, grad_rows, weight_blocks)
    residual_part = jnp.transpose(residual_part, (1, 0, 2)).reshape(part_tokens, model_width)
    columns = to_experts(columns)
    attn_part = jnp.transpose(columns, (1, 0, 2)).reshape(part_tokens, model_width)
    pre_part = (residual_part.astype(F32) + attn_part.astype(F32)).astype(BF16)
    pre_wide = pre_part.astype(F32)
    inv_part = lax.rsqrt(jnp.mean(pre_wide * pre_wide, axis=-1, keepdims=True) + 1e-06)
    inv_lanes = pad_lanes(split3(inv_part))
    pre_send = jnp.concatenate(
        [
            jnp.transpose(pre_part.reshape(part_tokens, group_count, slice_width), (1, 0, 2)),
            jnp.broadcast_to(inv_lanes[None], (group_count, part_tokens, 128)),
        ],
        2,
    )
    pre_back = lax.all_to_all(pre_send, GROUP, 0, 0, tiled=True).reshape(token_count, -1)
    pre_norm = pre_back[:, :slice_width].astype(F32)
    inv_scale = jnp.sum(pre_back[:, slice_width : slice_width + 3].astype(F32), axis=1, keepdims=True)
    unit_rows = pre_norm * inv_scale
    local_gain = lax.dynamic_slice_in_dim(norm_gain, group_place * slice_width, slice_width)
    normed = (unit_rows * local_gain).astype(BF16)

    expert_rows = group_gather(to_experts(dot(pick, normed).astype(BF16)))
    hidden_send = call(
        expert_kernel,
        shape(slot_total, 3 * hidden_width + LANES),
        1,
        0,
        scratch_shapes=buffers(*[(8, slot_total, slice_width)] * 2, (8, *block)),
    )(places, expert_rows, out_grad, weight_blocks)
    hidden_all = group_gather(hidden_send)
    grad_gate, grad_up, grad_down = call(
        weight_grad_kernel,
        [shape(model_width, hidden_width)] * 2 + [shape(hidden_width, model_width)],
    )(expert_rows, out_grad, hidden_send)
    grad_gate, grad_up, grad_down = grad_gate[None], grad_up[None], grad_down[None]
    back = call(
        project_kernel,
        shape(ctx_count, capacity, 2 * slice_width + LANES),
        1,
        0,
        scratch_shapes=buffers((8, slot_total, 3 * hidden_width + LANES), (8, *block)),
    )(places, hidden_all, *slice_weights)
    back = to_experts(back).reshape(slot_total, 2 * slice_width + LANES)

    routed = sum(
        dot(returns[k], back[:, :slice_width]) * mix_weight[:, k : k + 1] for k in range(top_count)
    )
    layer_out = (pre_norm + routed).astype(BF16)
    summed = dot(returns[0] + returns[1], back[:, slice_width:])
    normed_grad = summed[:, :slice_width].astype(BF16).astype(F32)
    center = jnp.sum(summed[:, slice_width : slice_width + 3], axis=1, keepdims=True) / model_width
    scaled_grad = normed_grad * local_gain
    grad_pre_norm = (
        grad_out.astype(F32) + inv_scale * (scaled_grad - unit_rows * center)
    ).astype(BF16)
    return (layer_out, grad_pre_norm, grad_gate, grad_up, grad_down)


def solution(mesh):
    placed = (
        P("ctx", ("role", "exp")),
        P("ctx", None),
        P(),
        P(("role", "exp"), None, None),
        P(("role", "exp"), "ctx"),
        P("ctx", ("role", "exp")),
        P(),
        P("ctx", None),
        P("ctx", None),
        P("ctx", None, ("role", "exp")),
        P("ctx", None, ("role", "exp")),
        P("ctx", ("role", "exp"), None),
        P("ctx", ("role", "exp")),
    )

    return jax.shard_map(
        per_device,
        mesh=mesh,
        in_specs=placed,
        out_specs=(
            P("ctx", ("role", "exp")),
            P("ctx", ("role", "exp")),
            P("ctx", None, ("role", "exp")),
            P("ctx", None, ("role", "exp")),
            P("ctx", ("role", "exp"), None),
        ),
        check_vma=False,
    )
```

```python
import functools

import jax
import jax.numpy as jnp
from jax import lax
from jax.experimental import pallas as pl
from jax.experimental.pallas import tpu as pltpu
from jax.sharding import PartitionSpec as P

ALL = ("ctx", "role", "exp")
GROUP = ("role", "exp")
BF16 = jnp.bfloat16
F32 = jnp.float32
SIDE = 4
LANES = 128


def dot(a, b, dims=((1,), (0,))):
    return lax.dot_general(a, b, (dims, ((), ())), preferred_element_type=F32)


def shift_z(block, step):
    return lax.ppermute(block, GROUP, [(g, (g + 2 * step) % 8) for g in range(8)])


def swap_core(block):
    return lax.ppermute(block, GROUP, [(g, g ^ 1) for g in range(8)])


def shift_plane(block, phase, step):
    pairs = []
    for c in range(SIDE * SIDE):
        x, y = divmod(c, SIDE)
        for g in range(8):
            if g % 2 == phase:
                to = x * SIDE + (y + step) % SIDE
            else:
                to = (x + step) % SIDE * SIDE + y
            pairs.append((c * 8 + g, to * 8 + g))
    return lax.ppermute(block, ALL, pairs)


def ctx_gather(block):
    for phase in range(2):
        block = jnp.stack([block] + [shift_plane(block, phase, -step) for step in range(1, SIDE)])
    return block


def group_gather(block):
    return lax.all_gather(block, GROUP, axis=0)


def group_exchange(blocks):
    received = [
        blocks[0],
        shift_z(blocks[3], -1),
        shift_z(blocks[2], 2),
        shift_z(blocks[1], 1),
    ]
    return [part for pair in received for part in (pair, swap_core(pair))]


def roll_lead(array, shift, axis):
    twice = jnp.concatenate([array, array], axis)
    return lax.dynamic_slice_in_dim(twice, shift, SIDE, axis)


def split3(value):
    high = lax.reduce_precision(value, 8, 7)
    rest = value - high
    middle = lax.reduce_precision(rest, 8, 7)
    low = lax.reduce_precision(rest - middle, 8, 7)
    return [term.astype(BF16) for term in (high, middle, low)]


def pad_lanes(terms):
    rows = terms[0].shape[0]
    blank = jnp.zeros((rows, LANES - len(terms)), BF16)
    return jnp.concatenate([t.reshape(rows, 1) for t in terms] + [blank], 1)


def lanes3(value, kind=BF16):
    lane = lax.broadcasted_iota(jnp.int32, (value.shape[0], LANES), 1)
    high = value.astype(BF16).astype(F32)
    rest = value - high
    middle = rest.astype(BF16).astype(F32)
    low = rest - middle
    wide = jnp.where(lane == 0, high, jnp.where(lane == 1, middle, jnp.where(lane == 2, low, 0.0)))
    return wide.astype(kind)


def call(kernel, outs, scalars=0, whole=None, **params):
    def run(*operands):
        count = len(operands) - scalars if whole is None else whole
        left = len(operands) - scalars - count
        spaces = [pltpu.SMEM] * scalars + [pltpu.VMEM] * count + [pl.ANY] * left
        return pl.pallas_call(
            kernel,
            out_shape=outs,
            in_specs=[pl.BlockSpec(memory_space=space) for space in spaces],
            **params,
        )(*operands)

    return run


def buffers(*shapes):
    return [pltpu.VMEM(shape, BF16) for shape in shapes] + [
        pltpu.SemaphoreType.DMA((len(shapes), shapes[0][0]))
    ]


def start_copies(lists, bufs, sems):
    copies = [
        [
            pltpu.make_async_copy(source, buf.at[place], sems.at[n, place])
            for place, source in enumerate(sources)
        ]
        for n, (sources, buf) in enumerate(zip(lists, bufs))
    ]
    for group in zip(*copies):
        for copy in group:
            copy.start()
    return copies


def member(place_ref, step, other):
    z = lax.rem(place_ref[0] + step, SIDE)
    return 2 * z + place_ref[1] + other - 2 * place_ref[1] * other


def prepare_kernel(place_ref, down_ref, gate_ref, up_ref, all_ref, *outs):
    slice_width = all_ref.shape[1]
    hidden = down_ref.shape[0]
    for place in range(8):
        step, other = place // 2, place % 2
        start = pl.multiple_of(member(place_ref, step, other) * slice_width, LANES)
        gate = gate_ref[pl.ds(start, slice_width), :]
        up = up_ref[pl.ds(start, slice_width), :]
        down = down_ref[:, pl.ds(start, slice_width)].T
        for at, ref in ((place, all_ref), (other, outs[step])):
            ref[at, :, :hidden] = gate
            ref[at, :, hidden : 2 * hidden] = up
            ref[at, :, 2 * hidden :] = down


def attend_kernel(scale, q_ref, near_ref, far_ref, key_frame_ref, own_frame_ref, uv_ref, out_ref):
    heads, latent_width, value_width = uv_ref.shape
    tokens = q_ref.shape[0]
    keys = [near_ref[...], far_ref[...]]
    count = keys[0].shape[0]
    query = jnp.concatenate(
        [q_ref[:, h * latent_width : (h + 1) * latent_width] for h in range(heads)], 0
    )
    own = own_frame_ref[...]
    scores = []
    for part in range(2):
        visible = key_frame_ref[:, part * count : (part + 1) * count] <= own
        visible = jnp.concatenate([visible.astype(F32)] * heads, 0) > 0.5
        scores.append(jnp.where(visible, dot(query, keys[part], ((1,), (1,))) * scale, -1e30))
    top = jnp.maximum(*[jnp.max(s, axis=1, keepdims=True) for s in scores])
    weights = [jnp.exp(s - top) for s in scores]
    total = sum(jnp.sum(w, axis=1, keepdims=True) for w in weights)
    mix = sum(dot(w.astype(BF16), k) for w, k in zip(weights, keys))
    mix = (mix / total).astype(BF16)
    for h in range(heads):
        out_ref[:, h * value_width : (h + 1) * value_width] = dot(
            mix[h * tokens : (h + 1) * tokens], uv_ref[h]
        ).astype(BF16)


def out_proj_kernel(rows_ref, weight_ref, *refs):
    out_ref, row_buf, weight_buf, sems = refs[-4:]
    members, columns, depth = weight_ref.shape
    copies = start_copies(
        [
            [rows_ref.at[:, :, pl.ds(p * depth, depth)] for p in range(members)],
            [weight_ref.at[p] for p in range(members)],
        ],
        [row_buf, weight_buf],
        sems,
    )
    total = jnp.zeros((rows_ref.shape[0] * rows_ref.shape[1], columns), F32)
    for place in range(members):
        for copy in copies:
            copy[place].wait()
        rows = row_buf[place].reshape(total.shape[0], depth)
        total = total + dot(rows, weight_buf[place], ((1,), (1,)))
    out_ref[...] = total.astype(BF16).reshape(out_ref.shape)


def expert_kernel(place_ref, rows_ref, grads_ref, weight_ref, out_ref, *scratch):
    row_buf, grad_buf, weight_buf, sems = scratch
    sources = [member(place_ref, p // 2, p % 2) for p in range(8)]
    copies = start_copies(
        [
            [grads_ref.at[source] for source in sources],
            [rows_ref.at[source] for source in sources],
            [weight_ref.at[p] for p in range(8)],
        ],
        [grad_buf, row_buf, weight_buf],
        sems,
    )
    hidden = weight_ref.shape[2] // 3
    both, hidden_grad = 0.0, 0.0
    for place in range(8):
        for copy in copies:
            copy[place].wait()
        both = both + dot(row_buf[place], weight_buf[place, :, : 2 * hidden])
        hidden_grad = hidden_grad + dot(grad_buf[place], weight_buf[place, :, 2 * hidden :])
    gate_in, up_in = both[:, :hidden], both[:, hidden:]
    gate_sig = 1.0 / (1.0 + jnp.exp(-gate_in))
    silu = gate_in * gate_sig
    gate_grad = hidden_grad * up_in * gate_sig * (1.0 + gate_in * (1.0 - gate_sig))
    up_grad = hidden_grad * silu
    center = jnp.sum(gate_grad * gate_in + up_grad * up_in, axis=1, keepdims=True)
    slots = gate_in.shape[0]
    out_ref[:slots, :hidden] = gate_grad.astype(BF16)
    out_ref[:slots, hidden : 2 * hidden] = up_grad.astype(BF16)
    out_ref[:slots, 2 * hidden :] = (silu * up_in).astype(BF16)
    out_ref[slots:, :] = jnp.zeros((out_ref.shape[0] - slots, 3 * hidden), BF16)
    out_ref[slots:, :slots] = lanes3(center, F32).T[: out_ref.shape[0] - slots].astype(BF16)


def weight_grad_kernel(rows_ref, grads_ref, hidden_ref, gate_ref, up_ref, down_ref):
    hidden = gate_ref.shape[1]
    members, _, slice_width = rows_ref.shape
    slots = rows_ref.shape[1]
    grads = hidden_ref[:slots, : 2 * hidden]
    units = hidden_ref[:slots, 2 * hidden :]
    for place in range(members):
        part = slice(place * slice_width, (place + 1) * slice_width)
        both = dot(rows_ref[place], grads, ((0,), (0,)))
        gate_ref[part, :] = both[:, :hidden].astype(BF16)
        up_ref[part, :] = both[:, hidden:].astype(BF16)
        down_ref[:, part] = dot(units, grads_ref[place], ((0,), (0,))).astype(BF16)


def project_kernel(place_ref, hidden_ref, *refs):
    weight_refs, out_ref, unit_buf, weight_buf, sems = refs[:8], *refs[8:]
    copies = start_copies(
        [
            [hidden_ref.at[member(place_ref, p // 2, p % 2)] for p in range(8)],
            [weight_refs[p].at[p % 2] for p in range(8)],
        ],
        [unit_buf, weight_buf],
        sems,
    )
    slice_width, wide = weight_refs[0].shape[1:]
    hidden = wide // 3
    slots = out_ref.shape[0] * out_ref.shape[1]
    rows, grads, center = 0.0, 0.0, 0.0
    for place in range(8):
        for copy in copies:
            copy[place].wait()
        units = unit_buf[place, :slots]
        weight = weight_buf[place]
        grads = grads + dot(units[:, : 2 * hidden], weight[:, : 2 * hidden], ((1,), (1,)))
        rows = rows + dot(units[:, 2 * hidden :], weight[:, 2 * hidden :], ((1,), (1,)))
        center = center + unit_buf[place, slots:].astype(F32)
    center = jnp.sum(center, axis=0, keepdims=True)
    center = jnp.broadcast_to(center, (LANES, wide)).T[:slots, :1]
    rows, grads, center = rows.astype(BF16), grads.astype(BF16), lanes3(center)
    sources, capacity = out_ref.shape[:2]
    for source in range(sources):
        part = slice(source * capacity, (source + 1) * capacity)
        out_ref[source, :, :slice_width] = rows[part]
        out_ref[source, :, slice_width : 2 * slice_width] = grads[part]
        out_ref[source, :, 2 * slice_width :] = center[part]


def per_device(
    queries,
    latent,
    frames,
    w_uv,
    w_out,
    residual,
    norm_gain,
    expert_ids,
    mix_codes,
    w_gate,
    w_up,
    w_down,
    grad_out,
):
    ctx_count = lax.axis_size("ctx")
    ctx_place = lax.axis_index("ctx")
    plane_x, plane_y = ctx_place // SIDE, ctx_place % SIDE
    group_place = lax.axis_index(GROUP)
    place_z, core = group_place // 2, group_place % 2
    group_count = 8
    token_count = queries.shape[0]
    head_count, latent_width, value_width = w_uv.shape
    model_width = w_gate.shape[1]
    slice_width = residual.shape[1]
    top_count = expert_ids.shape[1]
    hidden_width = w_gate.shape[2]
    column_width = w_out.shape[1]
    part_tokens = token_count // group_count
    capacity = token_count * top_count // ctx_count * 5 // 4
    slot_total = ctx_count * capacity

    def shape(*dims):
        return jax.ShapeDtypeStruct(dims, BF16)

    places = jnp.stack([place_z, core]).astype(jnp.int32)

    out_weight = group_gather(w_out.T)
    block = (slice_width, 3 * hidden_width)
    weight_blocks, *weight_pairs = call(
        prepare_kernel, [shape(8, *block)] + [shape(2, *block)] * SIDE, 1
    )(places, w_down[0], w_gate[0], w_up[0])

    residual_part = lax.all_to_all(
        residual.reshape(group_count, part_tokens, slice_width), GROUP, 0, 0, tiled=True
    )

    chosen = expert_ids.reshape(-1)
    pair_range = jnp.arange(token_count * top_count, dtype=jnp.int32)
    same = (chosen[:, None] == chosen[None, :]) & (pair_range[None, :] < pair_range[:, None])
    earlier = jnp.sum(same.astype(jnp.int32), axis=1)
    slot_index = (chosen * capacity + earlier).reshape(token_count, top_count)
    slot_range = jnp.arange(slot_total, dtype=jnp.int32)
    code_values = mix_codes.astype(F32)
    mix_weight = code_values / jnp.sum(code_values, axis=1, keepdims=True)
    hits = [slot_index[:, k][None, :] == slot_range[:, None] for k in range(top_count)]
    pick = sum(hit.astype(F32) for hit in hits).astype(BF16)
    slot_weight = sum(
        jnp.sum(jnp.where(hits[k], mix_weight[:, k][None, :], 0.0), axis=1) for k in range(top_count)
    )
    returns = [
        (slot_index[:, k][:, None] == slot_range[None, :]).astype(BF16) for k in range(top_count)
    ]

    def to_experts(rows):
        return lax.all_to_all(rows, "ctx", split_axis=0, concat_axis=0, tiled=True)

    grad_rows = (dot(pick, grad_out) * slot_weight[:, None]).astype(BF16)
    grad_rows = to_experts(grad_rows)
    out_grad = group_gather(grad_rows)
    slice_weights = group_exchange(weight_pairs)

    half = token_count // 2
    own_keys = ctx_gather(lax.dynamic_slice_in_dim(latent, core * half, half, 0))
    own_keys = own_keys.reshape(ctx_count * half, latent_width)
    other_keys = swap_core(own_keys)
    own_frames = lax.dynamic_slice_in_dim(frames, ctx_place * token_count, token_count)
    frame_grid = frames.reshape(SIDE, SIDE, 2, half)
    frame_grid = roll_lead(roll_lead(frame_grid, plane_x, 0), plane_y, 1)
    by_x = jnp.transpose(frame_grid, (2, 0, 1, 3))
    by_y = jnp.transpose(frame_grid, (2, 1, 0, 3))
    key_frames = jnp.where(
        core == 0,
        jnp.concatenate([by_x[0].reshape(-1), by_y[1].reshape(-1)]),
        jnp.concatenate([by_y[1].reshape(-1), by_x[0].reshape(-1)]),
    )
    heads = 4
    head_out = pl.pallas_call(
        functools.partial(attend_kernel, latent_width ** (-0.5)),
        out_shape=shape(token_count, head_count * value_width),
        grid=(head_count // heads,),
        in_specs=[
            pl.BlockSpec((token_count, heads * latent_width), lambda h: (0, h)),
            pl.BlockSpec(own_keys.shape, lambda h: (0, 0)),
            pl.BlockSpec(other_keys.shape, lambda h: (0, 0)),
            pl.BlockSpec((1, ctx_count * token_count), lambda h: (0, 0)),
            pl.BlockSpec((token_count, 1), lambda h: (0, 0)),
            pl.BlockSpec((heads, latent_width, value_width), lambda h: (h, 0, 0)),
        ],
        out_specs=pl.BlockSpec((token_count, heads * value_width), lambda h: (0, h)),
        name="attend",
    )(queries, own_keys, other_keys, key_frames[None], own_frames[:, None], w_uv)
    head_out = head_out.reshape(group_count, part_tokens, head_count * value_width)

    head_part = lax.all_to_all(head_out, GROUP, 0, 0, tiled=True)
    head_part = jnp.transpose(head_part, (1, 0, 2)).reshape(part_tokens, -1)
    all_heads = lax.all_gather(head_part, "ctx", axis=0)
    columns = call(
        out_proj_kernel,
        shape(ctx_count, part_tokens, column_width),
        whole=0,
        scratch_shapes=buffers(
            (group_count, ctx_count, part_tokens, head_count * value_width),
            (group_count, column_width, head_count * value_width),
        ),
    )(all_heads, out_weight, residual_part, grad_rows, weight_blocks)
    residual_part = jnp.transpose(residual_part, (1, 0, 2)).reshape(part_tokens, model_width)
    columns = to_experts(columns)
    attn_part = jnp.transpose(columns, (1, 0, 2)).reshape(part_tokens, model_width)
    pre_part = (residual_part.astype(F32) + attn_part.astype(F32)).astype(BF16)
    pre_wide = pre_part.astype(F32)
    inv_part = lax.rsqrt(jnp.mean(pre_wide * pre_wide, axis=-1, keepdims=True) + 1e-06)
    inv_lanes = pad_lanes(split3(inv_part))
    pre_send = jnp.concatenate(
        [
            jnp.transpose(pre_part.reshape(part_tokens, group_count, slice_width), (1, 0, 2)),
            jnp.broadcast_to(inv_lanes[None], (group_count, part_tokens, 128)),
        ],
        2,
    )
    pre_back = lax.all_to_all(pre_send, GROUP, 0, 0, tiled=True).reshape(token_count, -1)
    pre_norm = pre_back[:, :slice_width].astype(F32)
    inv_scale = jnp.sum(pre_back[:, slice_width : slice_width + 3].astype(F32), axis=1, keepdims=True)
    unit_rows = pre_norm * inv_scale
    local_gain = lax.dynamic_slice_in_dim(norm_gain, group_place * slice_width, slice_width)
    normed = (unit_rows * local_gain).astype(BF16)

    expert_rows = group_gather(to_experts(dot(pick, normed).astype(BF16)))
    hidden_send = call(
        expert_kernel,
        shape(slot_total + 8, 3 * hidden_width),
        1,
        0,
        scratch_shapes=buffers(*[(8, slot_total, slice_width)] * 2, (8, *block)),
    )(places, expert_rows, out_grad, weight_blocks)
    hidden_all = group_gather(hidden_send)
    grad_gate, grad_up, grad_down = call(
        weight_grad_kernel,
        [shape(model_width, hidden_width)] * 2 + [shape(hidden_width, model_width)],
    )(expert_rows, out_grad, hidden_send)
    grad_gate, grad_up, grad_down = grad_gate[None], grad_up[None], grad_down[None]
    back = call(
        project_kernel,
        shape(ctx_count, capacity, 2 * slice_width + LANES),
        1,
        0,
        scratch_shapes=buffers((8, slot_total + 8, 3 * hidden_width), (8, *block)),
    )(places, hidden_all, *slice_weights)
    back = to_experts(back).reshape(slot_total, 2 * slice_width + LANES)

    routed = sum(
        dot(returns[k], back[:, :slice_width]) * mix_weight[:, k : k + 1] for k in range(top_count)
    )
    layer_out = (pre_norm + routed).astype(BF16)
    summed = dot(returns[0] + returns[1], back[:, slice_width:])
    normed_grad = summed[:, :slice_width].astype(BF16).astype(F32)
    center = jnp.sum(summed[:, slice_width : slice_width + 3], axis=1, keepdims=True) / model_width
    scaled_grad = normed_grad * local_gain
    grad_pre_norm = (
        grad_out.astype(F32) + inv_scale * (scaled_grad - unit_rows * center)
    ).astype(BF16)
    return (layer_out, grad_pre_norm, grad_gate, grad_up, grad_down)


def solution(mesh):
    placed = (
        P("ctx", ("role", "exp")),
        P("ctx", None),
        P(),
        P(("role", "exp"), None, None),
        P(("role", "exp"), "ctx"),
        P("ctx", ("role", "exp")),
        P(),
        P("ctx", None),
        P("ctx", None),
        P("ctx", None, ("role", "exp")),
        P("ctx", None, ("role", "exp")),
        P("ctx", ("role", "exp"), None),
        P("ctx", ("role", "exp")),
    )

    return jax.shard_map(
        per_device,
        mesh=mesh,
        in_specs=placed,
        out_specs=(
            P("ctx", ("role", "exp")),
            P("ctx", ("role", "exp")),
            P("ctx", None, ("role", "exp")),
            P("ctx", None, ("role", "exp")),
            P("ctx", ("role", "exp"), None),
        ),
        check_vma=False,
    )
```

```python
import functools

import jax
import jax.numpy as jnp
from jax import lax
from jax.experimental import pallas as pl
from jax.experimental.pallas import tpu as pltpu
from jax.sharding import PartitionSpec as P

ALL = ("ctx", "role", "exp")
GROUP = ("role", "exp")
BF16 = jnp.bfloat16
F32 = jnp.float32
SIDE = 4
LANES = 128


def dot(a, b, dims=((1,), (0,))):
    return lax.dot_general(a, b, (dims, ((), ())), preferred_element_type=F32)


def shift_z(block, step):
    return lax.ppermute(block, GROUP, [(g, (g + 2 * step) % 8) for g in range(8)])


def swap_core(block):
    return lax.ppermute(block, GROUP, [(g, g ^ 1) for g in range(8)])


def shift_plane(block, phase, step):
    pairs = []
    for c in range(SIDE * SIDE):
        x, y = divmod(c, SIDE)
        for g in range(8):
            if g % 2 == phase:
                to = x * SIDE + (y + step) % SIDE
            else:
                to = (x + step) % SIDE * SIDE + y
            pairs.append((c * 8 + g, to * 8 + g))
    return lax.ppermute(block, ALL, pairs)


def direct_ring(block, phase):
    others = [shift_plane(block, phase, -step) for step in range(1, SIDE)]
    return jnp.stack([block] + others)


def halves_ring(block, phase):
    half = block.shape[0] // 2
    before = shift_plane(block, phase, 1)
    after = shift_plane(block, phase, -1)
    far = [shift_plane(before[:half], phase, 1), shift_plane(after[half:], phase, -1)]
    return [block, after, *far, before]


def group_gather(block):
    return lax.all_gather(block, GROUP, axis=0)


def group_exchange(blocks):
    received = [
        blocks[0],
        shift_z(blocks[3], -1),
        shift_z(blocks[2], 2),
        shift_z(blocks[1], 1),
    ]
    return [part for pair in received for part in (pair, swap_core(pair))]


def roll_lead(array, shift, axis):
    twice = jnp.concatenate([array, array], axis)
    return lax.dynamic_slice_in_dim(twice, shift, SIDE, axis)


def split3(value):
    high = lax.reduce_precision(value, 8, 7)
    rest = value - high
    middle = lax.reduce_precision(rest, 8, 7)
    low = lax.reduce_precision(rest - middle, 8, 7)
    return [term.astype(BF16) for term in (high, middle, low)]


def pad_lanes(terms):
    rows = terms[0].shape[0]
    blank = jnp.zeros((rows, LANES - len(terms)), BF16)
    return jnp.concatenate([t.reshape(rows, 1) for t in terms] + [blank], 1)


def lanes3(value, kind=BF16):
    lane = lax.broadcasted_iota(jnp.int32, (value.shape[0], LANES), 1)
    high = value.astype(BF16).astype(F32)
    rest = value - high
    middle = rest.astype(BF16).astype(F32)
    low = rest - middle
    wide = jnp.where(lane == 0, high, jnp.where(lane == 1, middle, jnp.where(lane == 2, low, 0.0)))
    return wide.astype(kind)


def call(kernel, outs, scalars=0, whole=None, **params):
    def run(*operands):
        count = len(operands) - scalars if whole is None else whole
        left = len(operands) - scalars - count
        spaces = [pltpu.SMEM] * scalars + [pltpu.VMEM] * count + [pl.ANY] * left
        return pl.pallas_call(
            kernel,
            out_shape=outs,
            in_specs=[pl.BlockSpec(memory_space=space) for space in spaces],
            **params,
        )(*operands)

    return run


def buffers(*shapes):
    return [pltpu.VMEM(shape, BF16) for shape in shapes] + [
        pltpu.SemaphoreType.DMA((len(shapes), shapes[0][0]))
    ]


def start_copies(lists, bufs, sems):
    copies = [
        [
            pltpu.make_async_copy(source, buf.at[place], sems.at[n, place])
            for place, source in enumerate(sources)
        ]
        for n, (sources, buf) in enumerate(zip(lists, bufs))
    ]
    for group in zip(*copies):
        for copy in group:
            copy.start()
    return copies


def member(place_ref, step, other):
    z = lax.rem(place_ref[0] + step, SIDE)
    return 2 * z + place_ref[1] + other - 2 * place_ref[1] * other


def prepare_kernel(place_ref, down_ref, gate_ref, up_ref, all_ref, *outs):
    slice_width = all_ref.shape[1]
    hidden = down_ref.shape[0]
    for place in range(8):
        step, other = place // 2, place % 2
        start = pl.multiple_of(member(place_ref, step, other) * slice_width, LANES)
        gate = gate_ref[pl.ds(start, slice_width), :]
        up = up_ref[pl.ds(start, slice_width), :]
        down = down_ref[:, pl.ds(start, slice_width)].T
        for at, ref in ((place, all_ref), (other, outs[step])):
            ref[at, :, :hidden] = gate
            ref[at, :, hidden : 2 * hidden] = up
            ref[at, :, 2 * hidden :] = down


def attend_kernel(scale, q_ref, near_ref, far_ref, key_frame_ref, own_frame_ref, uv_ref, out_ref):
    heads, latent_width, value_width = uv_ref.shape
    tokens = q_ref.shape[0]
    keys = [near_ref[...], far_ref[...]]
    count = keys[0].shape[0]
    query = jnp.concatenate(
        [q_ref[:, h * latent_width : (h + 1) * latent_width] for h in range(heads)], 0
    )
    own = own_frame_ref[...]
    scores = []
    for part in range(2):
        visible = key_frame_ref[:, part * count : (part + 1) * count] <= own
        visible = jnp.concatenate([visible.astype(F32)] * heads, 0) > 0.5
        scores.append(jnp.where(visible, dot(query, keys[part], ((1,), (1,))) * scale, -1e30))
    top = jnp.maximum(*[jnp.max(s, axis=1, keepdims=True) for s in scores])
    weights = [jnp.exp(s - top) for s in scores]
    total = sum(jnp.sum(w, axis=1, keepdims=True) for w in weights)
    mix = sum(dot(w.astype(BF16), k) for w, k in zip(weights, keys))
    mix = (mix / total).astype(BF16)
    for h in range(heads):
        out_ref[:, h * value_width : (h + 1) * value_width] = dot(
            mix[h * tokens : (h + 1) * tokens], uv_ref[h]
        ).astype(BF16)


def out_proj_kernel(place_ref, *refs):
    piece_refs, weight_ref, out_ref, row_buf, weight_buf, sems = refs[:5], *refs[5:]
    members, columns, depth = weight_ref.shape
    copies = []
    for place in range(members):
        part = pl.ds(place * depth, depth)
        group = [pltpu.make_async_copy(weight_ref.at[place], weight_buf.at[place], sems.at[place, 0])]
        first = 0
        for n, ref in enumerate(piece_refs):
            count = ref.shape[0]
            group.append(
                pltpu.make_async_copy(
                    ref.at[:, :, part],
                    row_buf.at[place, pl.ds(first, count)],
                    sems.at[place, n + 1],
                )
            )
            first += count
        for copy in group:
            copy.start()
        copies.append(group)
    tokens = out_ref.shape[1]
    total = jnp.zeros((SIDE * SIDE * tokens, columns), F32)
    for place in range(members):
        for copy in copies[place]:
            copy.wait()
        rows = row_buf[place].reshape(total.shape[0], depth)
        total = total + dot(rows, weight_buf[place], ((1,), (1,)))
    total = total.astype(BF16)
    core = place_ref[1]
    for i in range(SIDE):
        for j in range(SIDE):
            step_x = i + core * (j - i)
            step_y = j + core * (i - j)
            owner = lax.rem(place_ref[2] + step_x, SIDE) * SIDE + lax.rem(
                place_ref[3] + step_y, SIDE
            )
            first = (i * SIDE + j) * tokens
            out_ref[owner] = total[first : first + tokens]


def expert_kernel(place_ref, rows_ref, grads_ref, weight_ref, out_ref, *scratch):
    row_buf, grad_buf, weight_buf, sems = scratch
    sources = [member(place_ref, p // 2, p % 2) for p in range(8)]
    copies = start_copies(
        [
            [grads_ref.at[source] for source in sources],
            [rows_ref.at[source] for source in sources],
            [weight_ref.at[p] for p in range(8)],
        ],
        [grad_buf, row_buf, weight_buf],
        sems,
    )
    hidden = weight_ref.shape[2] // 3
    both, hidden_grad = 0.0, 0.0
    for place in range(8):
        for copy in copies:
            copy[place].wait()
        both = both + dot(row_buf[place], weight_buf[place, :, : 2 * hidden])
        hidden_grad = hidden_grad + dot(grad_buf[place], weight_buf[place, :, 2 * hidden :])
    gate_in, up_in = both[:, :hidden], both[:, hidden:]
    gate_sig = 1.0 / (1.0 + jnp.exp(-gate_in))
    silu = gate_in * gate_sig
    gate_grad = hidden_grad * up_in * gate_sig * (1.0 + gate_in * (1.0 - gate_sig))
    up_grad = hidden_grad * silu
    center = jnp.sum(gate_grad * gate_in + up_grad * up_in, axis=1, keepdims=True)
    slots = gate_in.shape[0]
    out_ref[:slots, :hidden] = gate_grad.astype(BF16)
    out_ref[:slots, hidden : 2 * hidden] = up_grad.astype(BF16)
    out_ref[:slots, 2 * hidden :] = (silu * up_in).astype(BF16)
    out_ref[slots:, :] = jnp.zeros((out_ref.shape[0] - slots, 3 * hidden), BF16)
    out_ref[slots:, :slots] = lanes3(center, F32).T[: out_ref.shape[0] - slots].astype(BF16)


def weight_grad_kernel(rows_ref, grads_ref, hidden_ref, gate_ref, up_ref, down_ref):
    hidden = gate_ref.shape[1]
    members, _, slice_width = rows_ref.shape
    slots = rows_ref.shape[1]
    grads = hidden_ref[:slots, : 2 * hidden]
    units = hidden_ref[:slots, 2 * hidden :]

    def block(place, carry):
        part = pl.ds(pl.multiple_of(place * slice_width, LANES), slice_width)
        both = dot(rows_ref[place], grads, ((0,), (0,)))
        gate_ref[part, :] = both[:, :hidden].astype(BF16)
        up_ref[part, :] = both[:, hidden:].astype(BF16)
        down_ref[:, part] = dot(units, grads_ref[place], ((0,), (0,))).astype(BF16)
        return carry

    lax.fori_loop(0, members, block, 0)


def project_kernel(place_ref, hidden_ref, *refs):
    weight_refs, out_ref, unit_buf, weight_buf, sems = refs[:8], *refs[8:]
    copies = start_copies(
        [
            [hidden_ref.at[member(place_ref, p // 2, p % 2)] for p in range(8)],
            [weight_refs[p].at[p % 2] for p in range(8)],
        ],
        [unit_buf, weight_buf],
        sems,
    )
    slice_width, wide = weight_refs[0].shape[1:]
    hidden = wide // 3
    slots = out_ref.shape[0] * out_ref.shape[1]
    rows, grads, center = 0.0, 0.0, 0.0
    for place in range(8):
        for copy in copies:
            copy[place].wait()
        units = unit_buf[place, :slots]
        weight = weight_buf[place]
        grads = grads + dot(units[:, : 2 * hidden], weight[:, : 2 * hidden], ((1,), (1,)))
        rows = rows + dot(units[:, 2 * hidden :], weight[:, 2 * hidden :], ((1,), (1,)))
        center = center + unit_buf[place, slots:].astype(F32)
    center = jnp.sum(center, axis=0, keepdims=True)
    center = jnp.broadcast_to(center, (LANES, wide)).T[:slots, :1]
    rows, grads, center = rows.astype(BF16), grads.astype(BF16), lanes3(center)
    sources, capacity = out_ref.shape[:2]
    for source in range(sources):
        part = slice(source * capacity, (source + 1) * capacity)
        out_ref[source, :, :slice_width] = rows[part]
        out_ref[source, :, slice_width : 2 * slice_width] = grads[part]
        out_ref[source, :, 2 * slice_width :] = center[part]


def per_device(
    queries,
    latent,
    frames,
    w_uv,
    w_out,
    residual,
    norm_gain,
    expert_ids,
    mix_codes,
    w_gate,
    w_up,
    w_down,
    grad_out,
):
    ctx_count = lax.axis_size("ctx")
    ctx_place = lax.axis_index("ctx")
    plane_x, plane_y = ctx_place // SIDE, ctx_place % SIDE
    group_place = lax.axis_index(GROUP)
    place_z, core = group_place // 2, group_place % 2
    group_count = 8
    token_count = queries.shape[0]
    head_count, latent_width, value_width = w_uv.shape
    model_width = w_gate.shape[1]
    slice_width = residual.shape[1]
    top_count = expert_ids.shape[1]
    hidden_width = w_gate.shape[2]
    column_width = w_out.shape[1]
    part_tokens = token_count // group_count
    capacity = token_count * top_count // ctx_count * 5 // 4
    slot_total = ctx_count * capacity

    def shape(*dims):
        return jax.ShapeDtypeStruct(dims, BF16)

    places = jnp.stack([place_z, core, plane_x, plane_y]).astype(jnp.int32)

    out_weight = group_gather(w_out.T)
    block = (slice_width, 3 * hidden_width)
    weight_blocks, *weight_pairs = call(
        prepare_kernel, [shape(8, *block)] + [shape(2, *block)] * SIDE, 1
    )(places, w_down[0], w_gate[0], w_up[0])

    chosen = expert_ids.reshape(-1)
    pair_range = jnp.arange(token_count * top_count, dtype=jnp.int32)
    same = (chosen[:, None] == chosen[None, :]) & (pair_range[None, :] < pair_range[:, None])
    earlier = jnp.sum(same.astype(jnp.int32), axis=1)
    slot_index = (chosen * capacity + earlier).reshape(token_count, top_count)
    slot_range = jnp.arange(slot_total, dtype=jnp.int32)
    code_values = mix_codes.astype(F32)
    mix_weight = code_values / jnp.sum(code_values, axis=1, keepdims=True)
    hits = [slot_index[:, k][None, :] == slot_range[:, None] for k in range(top_count)]
    pick = sum(hit.astype(F32) for hit in hits).astype(BF16)
    slot_weight = sum(
        jnp.sum(jnp.where(hits[k], mix_weight[:, k][None, :], 0.0), axis=1) for k in range(top_count)
    )
    returns = [
        (slot_index[:, k][:, None] == slot_range[None, :]).astype(BF16) for k in range(top_count)
    ]

    def to_experts(rows):
        return lax.all_to_all(rows, "ctx", split_axis=0, concat_axis=0, tiled=True)

    grad_rows = (dot(pick, grad_out) * slot_weight[:, None]).astype(BF16)
    grad_rows = to_experts(grad_rows)
    out_grad = group_gather(grad_rows)
    slice_weights = group_exchange(weight_pairs)

    half = token_count // 2
    own_keys = lax.dynamic_slice_in_dim(latent, core * half, half, 0)
    own_frames = lax.dynamic_slice_in_dim(frames, ctx_place * token_count, token_count)
    frame_grid = frames.reshape(SIDE, SIDE, 2, half)
    frame_grid = roll_lead(roll_lead(frame_grid, plane_x, 0), plane_y, 1)
    by_x = jnp.transpose(frame_grid, (2, 0, 1, 3))
    by_y = jnp.transpose(frame_grid, (2, 1, 0, 3))
    key_frames = jnp.where(
        core == 0,
        jnp.concatenate([by_x[0].reshape(-1), by_y[1].reshape(-1)]),
        jnp.concatenate([by_y[1].reshape(-1), by_x[0].reshape(-1)]),
    )
    own_keys = direct_ring(own_keys, 0)
    own_keys, key_frames, own_frames = lax.optimization_barrier(
        (own_keys, key_frames[None], own_frames[:, None])
    )
    own_keys = direct_ring(own_keys, 1)
    own_keys = own_keys.reshape(ctx_count * half, latent_width)
    other_keys = swap_core(own_keys)
    heads = 4
    head_out = pl.pallas_call(
        functools.partial(attend_kernel, latent_width ** (-0.5)),
        out_shape=shape(token_count, head_count * value_width),
        grid=(head_count // heads,),
        in_specs=[
            pl.BlockSpec((token_count, heads * latent_width), lambda h: (0, h)),
            pl.BlockSpec(own_keys.shape, lambda h: (0, 0)),
            pl.BlockSpec(other_keys.shape, lambda h: (0, 0)),
            pl.BlockSpec((1, ctx_count * token_count), lambda h: (0, 0)),
            pl.BlockSpec((token_count, 1), lambda h: (0, 0)),
            pl.BlockSpec((heads, latent_width, value_width), lambda h: (h, 0, 0)),
        ],
        out_specs=pl.BlockSpec((token_count, heads * value_width), lambda h: (0, h)),
        name="attend",
    )(queries, own_keys, other_keys, key_frames, own_frames, w_uv)
    head_out = head_out.reshape(group_count, part_tokens, head_count * value_width)

    head_width = head_count * value_width
    exchange = jnp.concatenate(
        [head_out, residual.reshape(group_count, part_tokens, slice_width)], 2
    )
    exchange = lax.all_to_all(exchange, GROUP, 0, 0, tiled=True)
    exchange = jnp.transpose(exchange, (1, 0, 2))
    head_part = exchange[:, :, :head_width].reshape(part_tokens, -1)
    residual_part = exchange[:, :, head_width:].reshape(part_tokens, model_width)
    pieces = halves_ring(direct_ring(head_part, 0), 1)
    columns = call(
        out_proj_kernel,
        shape(ctx_count, part_tokens, column_width),
        1,
        whole=0,
        scratch_shapes=[
            pltpu.VMEM((group_count, ctx_count, part_tokens, head_width), BF16),
            pltpu.VMEM((group_count, column_width, head_width), BF16),
            pltpu.SemaphoreType.DMA((group_count, len(pieces) + 1)),
        ],
    )(places, *pieces, out_weight)
    columns = to_experts(columns)
    attn_part = jnp.transpose(columns, (1, 0, 2)).reshape(part_tokens, model_width)
    pre_part = (residual_part.astype(F32) + attn_part.astype(F32)).astype(BF16)
    pre_wide = pre_part.astype(F32)
    inv_part = lax.rsqrt(jnp.mean(pre_wide * pre_wide, axis=-1, keepdims=True) + 1e-06)
    inv_lanes = pad_lanes(split3(inv_part))
    pre_send = jnp.concatenate(
        [
            jnp.transpose(pre_part.reshape(part_tokens, group_count, slice_width), (1, 0, 2)),
            jnp.broadcast_to(inv_lanes[None], (group_count, part_tokens, 128)),
        ],
        2,
    )
    pre_back = lax.all_to_all(pre_send, GROUP, 0, 0, tiled=True).reshape(token_count, -1)
    pre_norm = pre_back[:, :slice_width].astype(F32)
    inv_scale = jnp.sum(pre_back[:, slice_width : slice_width + 3].astype(F32), axis=1, keepdims=True)
    unit_rows = pre_norm * inv_scale
    local_gain = lax.dynamic_slice_in_dim(norm_gain, group_place * slice_width, slice_width)
    normed = (unit_rows * local_gain).astype(BF16)

    expert_rows = group_gather(to_experts(dot(pick, normed).astype(BF16)))
    hidden_send = call(
        expert_kernel,
        shape(slot_total + 8, 3 * hidden_width),
        1,
        0,
        scratch_shapes=buffers(*[(8, slot_total, slice_width)] * 2, (8, *block)),
    )(places, expert_rows, out_grad, weight_blocks)
    hidden_all = group_gather(hidden_send)
    grad_gate, grad_up, grad_down = call(
        weight_grad_kernel,
        [shape(model_width, hidden_width)] * 2 + [shape(hidden_width, model_width)],
    )(expert_rows, out_grad, hidden_send)
    grad_gate, grad_up, grad_down = grad_gate[None], grad_up[None], grad_down[None]
    back = call(
        project_kernel,
        shape(ctx_count, capacity, 2 * slice_width + LANES),
        1,
        0,
        scratch_shapes=buffers((8, slot_total + 8, 3 * hidden_width), (8, *block)),
    )(places, hidden_all, *slice_weights)
    back = to_experts(back).reshape(slot_total, 2 * slice_width + LANES)

    routed = sum(
        dot(returns[k], back[:, :slice_width]) * mix_weight[:, k : k + 1] for k in range(top_count)
    )
    layer_out = (pre_norm + routed).astype(BF16)
    summed = dot(returns[0] + returns[1], back[:, slice_width:])
    normed_grad = summed[:, :slice_width].astype(BF16).astype(F32)
    center = jnp.sum(summed[:, slice_width : slice_width + 3], axis=1, keepdims=True) / model_width
    scaled_grad = normed_grad * local_gain
    grad_pre_norm = (
        grad_out.astype(F32) + inv_scale * (scaled_grad - unit_rows * center)
    ).astype(BF16)
    return (layer_out, grad_pre_norm, grad_gate, grad_up, grad_down)


def solution(mesh):
    placed = (
        P("ctx", ("role", "exp")),
        P("ctx", None),
        P(),
        P(("role", "exp"), None, None),
        P(("role", "exp"), "ctx"),
        P("ctx", ("role", "exp")),
        P(),
        P("ctx", None),
        P("ctx", None),
        P("ctx", None, ("role", "exp")),
        P("ctx", None, ("role", "exp")),
        P("ctx", ("role", "exp"), None),
        P("ctx", ("role", "exp")),
    )

    return jax.shard_map(
        per_device,
        mesh=mesh,
        in_specs=placed,
        out_specs=(
            P("ctx", ("role", "exp")),
            P("ctx", ("role", "exp")),
            P("ctx", None, ("role", "exp")),
            P("ctx", None, ("role", "exp")),
            P("ctx", ("role", "exp"), None),
        ),
        check_vma=False,
    )
```

```python
import functools

import jax
import jax.numpy as jnp
from jax import lax
from jax.experimental import pallas as pl
from jax.experimental.pallas import tpu as pltpu
from jax.sharding import PartitionSpec as P

ALL = ("ctx", "role", "exp")
GROUP = ("role", "exp")
BF16 = jnp.bfloat16
F32 = jnp.float32
SIDE = 4
LANES = 128


def dot(a, b, dims=((1,), (0,))):
    return lax.dot_general(a, b, (dims, ((), ())), preferred_element_type=F32)


def shift_z(block, step):
    return lax.ppermute(block, GROUP, [(g, (g + 2 * step) % 8) for g in range(8)])


def swap_core(block):
    return lax.ppermute(block, GROUP, [(g, g ^ 1) for g in range(8)])


def shift_plane(block, phase, step):
    pairs = []
    for c in range(SIDE * SIDE):
        x, y = divmod(c, SIDE)
        for g in range(8):
            if g % 2 == phase:
                to = x * SIDE + (y + step) % SIDE
            else:
                to = (x + step) % SIDE * SIDE + y
            pairs.append((c * 8 + g, to * 8 + g))
    return lax.ppermute(block, ALL, pairs)


def direct_ring(block, phase):
    others = [shift_plane(block, phase, -step) for step in range(1, SIDE)]
    return jnp.stack([block] + others)


def halves_ring(block, phase):
    half = block.shape[0] // 2
    before = shift_plane(block, phase, 1)
    after = shift_plane(block, phase, -1)
    far = [shift_plane(before[:half], phase, 1), shift_plane(after[half:], phase, -1)]
    return [block, after, *far, before]


def group_gather(block):
    return lax.all_gather(block, GROUP, axis=0)


def group_exchange(blocks):
    received = [
        blocks[0],
        shift_z(blocks[3], -1),
        shift_z(blocks[2], 2),
        shift_z(blocks[1], 1),
    ]
    return [part for pair in received for part in (pair, swap_core(pair))]


def roll_lead(array, shift, axis):
    twice = jnp.concatenate([array, array], axis)
    return lax.dynamic_slice_in_dim(twice, shift, SIDE, axis)


def split3(value):
    high = lax.reduce_precision(value, 8, 7)
    rest = value - high
    middle = lax.reduce_precision(rest, 8, 7)
    low = lax.reduce_precision(rest - middle, 8, 7)
    return [term.astype(BF16) for term in (high, middle, low)]


def pad_lanes(terms):
    rows = terms[0].shape[0]
    blank = jnp.zeros((rows, LANES - len(terms)), BF16)
    return jnp.concatenate([t.reshape(rows, 1) for t in terms] + [blank], 1)


def lanes3(value, kind=BF16, first=0):
    lane = lax.broadcasted_iota(jnp.int32, (value.shape[0], LANES), 1) - first
    high = value.astype(BF16).astype(F32)
    rest = value - high
    middle = rest.astype(BF16).astype(F32)
    low = rest - middle
    wide = jnp.where(lane == 0, high, jnp.where(lane == 1, middle, jnp.where(lane == 2, low, 0.0)))
    return wide.astype(kind)


def call(kernel, outs, scalars=0, whole=None, **params):
    def run(*operands):
        count = len(operands) - scalars if whole is None else whole
        left = len(operands) - scalars - count
        spaces = [pltpu.SMEM] * scalars + [pltpu.VMEM] * count + [pl.ANY] * left
        return pl.pallas_call(
            kernel,
            out_shape=outs,
            in_specs=[pl.BlockSpec(memory_space=space) for space in spaces],
            **params,
        )(*operands)

    return run


def buffers(*shapes):
    return [pltpu.VMEM(shape, BF16) for shape in shapes] + [
        pltpu.SemaphoreType.DMA((len(shapes), shapes[0][0]))
    ]


def start_copies(lists, bufs, sems):
    copies = [
        [
            pltpu.make_async_copy(source, buf.at[place], sems.at[n, place])
            for place, source in enumerate(sources)
        ]
        for n, (sources, buf) in enumerate(zip(lists, bufs))
    ]
    for group in zip(*copies):
        for copy in group:
            copy.start()
    return copies


def member(place_ref, step, other):
    z = lax.rem(place_ref[0] + step, SIDE)
    return 2 * z + place_ref[1] + other - 2 * place_ref[1] * other


def prepare_kernel(place_ref, down_ref, gate_ref, up_ref, all_ref, *outs):
    slice_width = all_ref.shape[1]
    hidden = down_ref.shape[0]
    for place in range(8):
        step, other = place // 2, place % 2
        start = pl.multiple_of(member(place_ref, step, other) * slice_width, LANES)
        gate = gate_ref[pl.ds(start, slice_width), :]
        up = up_ref[pl.ds(start, slice_width), :]
        down = down_ref[:, pl.ds(start, slice_width)].T
        for at, ref in ((place, all_ref), (other, outs[step])):
            ref[at, :, :hidden] = gate
            ref[at, :, hidden : 2 * hidden] = up
            ref[at, :, 2 * hidden :] = down


def attend_kernel(scale, q_ref, near_ref, far_ref, key_frame_ref, own_frame_ref, uv_ref, out_ref):
    heads, latent_width, value_width = uv_ref.shape
    tokens = q_ref.shape[0]
    keys = [near_ref[...], far_ref[...]]
    count = keys[0].shape[0]
    query = jnp.concatenate(
        [q_ref[:, h * latent_width : (h + 1) * latent_width] for h in range(heads)], 0
    )
    own = own_frame_ref[...]
    scores = []
    for part in range(2):
        visible = key_frame_ref[:, part * count : (part + 1) * count] <= own
        visible = jnp.concatenate([visible.astype(F32)] * heads, 0) > 0.5
        scores.append(jnp.where(visible, dot(query, keys[part], ((1,), (1,))) * scale, -1e30))
    top = jnp.maximum(*[jnp.max(s, axis=1, keepdims=True) for s in scores])
    weights = [jnp.exp(s - top) for s in scores]
    total = sum(jnp.sum(w, axis=1, keepdims=True) for w in weights)
    mix = sum(dot(w.astype(BF16), k) for w, k in zip(weights, keys))
    mix = (mix / total).astype(BF16)
    for h in range(heads):
        out_ref[:, h * value_width : (h + 1) * value_width] = dot(
            mix[h * tokens : (h + 1) * tokens], uv_ref[h]
        ).astype(BF16)


def out_proj_kernel(place_ref, *refs):
    weight_refs, piece_refs, out_ref, *bufs = refs[:2], refs[2:7], *refs[7:]
    piece_bufs, sems = bufs[:5], bufs[5]
    copies = [
        pltpu.make_async_copy(ref, buf, sems.at[n])
        for n, (ref, buf) in enumerate(zip(piece_refs, piece_bufs))
    ]
    for copy in copies:
        copy.start()
    tokens = out_ref.shape[1]
    core = place_ref[1]
    block = 0
    for copy, buf in zip(copies, piece_bufs):
        copy.wait()
        total = 0.0
        for other in range(2):
            rows = buf[:, other].reshape(buf.shape[0] * tokens, buf.shape[3])
            total = total + dot(rows, weight_refs[other][...], ((1,), (1,)))
        total = total.astype(BF16)
        for n in range(buf.shape[0]):
            i, j = block // SIDE, block % SIDE
            step_x = i + core * (j - i)
            step_y = j + core * (i - j)
            owner = lax.rem(place_ref[2] + step_x, SIDE) * SIDE + lax.rem(
                place_ref[3] + step_y, SIDE
            )
            out_ref[owner] = total[n * tokens : (n + 1) * tokens]
            block += 1


def expert_kernel(place_ref, rows_ref, grads_ref, weight_ref, out_ref, scaled_ref, scale_ref, *scratch):
    row_buf, grad_buf, weight_buf, sems = scratch
    sources = [member(place_ref, p // 2, p % 2) for p in range(8)]
    copies = start_copies(
        [
            [grads_ref.at[source] for source in sources],
            [rows_ref.at[source] for source in sources],
            [weight_ref.at[p] for p in range(8)],
        ],
        [grad_buf, row_buf, weight_buf],
        sems,
    )
    hidden = weight_ref.shape[2] // 3
    width = weight_ref.shape[1]
    both, hidden_grad, square = 0.0, 0.0, 0.0
    for place in range(8):
        for copy in copies:
            copy[place].wait()
        both = both + dot(row_buf[place, :, :width], weight_buf[place, :, : 2 * hidden])
        square = square + row_buf[place, :, width:].astype(F32)
        hidden_grad = hidden_grad + dot(grad_buf[place], weight_buf[place, :, 2 * hidden :])
    square = jnp.sum(square, axis=1, keepdims=True)
    inv_scale = lax.rsqrt(square / (8 * width) + 1e-06)
    gate_in, up_in = both[:, :hidden] * inv_scale, both[:, hidden:] * inv_scale
    gate_sig = 1.0 / (1.0 + jnp.exp(-gate_in))
    silu = gate_in * gate_sig
    gate_grad = hidden_grad * up_in * gate_sig * (1.0 + gate_in * (1.0 - gate_sig))
    up_grad = hidden_grad * silu
    center = jnp.sum(gate_grad * gate_in + up_grad * up_in, axis=1, keepdims=True)
    slots = gate_in.shape[0]
    scaled_ref[:, :hidden] = (gate_grad * inv_scale).astype(BF16)
    scaled_ref[:, hidden:] = (up_grad * inv_scale).astype(BF16)
    scale_ref[...] = lanes3(inv_scale, first=3)
    out_ref[:slots, :hidden] = gate_grad.astype(BF16)
    out_ref[:slots, hidden : 2 * hidden] = up_grad.astype(BF16)
    out_ref[:slots, 2 * hidden :] = (silu * up_in).astype(BF16)
    out_ref[slots:, :] = jnp.zeros((out_ref.shape[0] - slots, 3 * hidden), BF16)
    out_ref[slots:, :slots] = lanes3(center, F32).T[: out_ref.shape[0] - slots].astype(BF16)


def weight_grad_kernel(rows_ref, grads_ref, hidden_ref, scaled_ref, gate_ref, up_ref, down_ref):
    hidden = gate_ref.shape[1]
    members, slots, slice_width = grads_ref.shape
    grads = scaled_ref[...]
    units = hidden_ref[:slots, 2 * hidden :]

    def block(place, carry):
        part = pl.ds(pl.multiple_of(place * slice_width, LANES), slice_width)
        both = dot(rows_ref[place, :, :slice_width], grads, ((0,), (0,)))
        gate_ref[part, :] = both[:, :hidden].astype(BF16)
        up_ref[part, :] = both[:, hidden:].astype(BF16)
        down_ref[:, part] = dot(units, grads_ref[place], ((0,), (0,))).astype(BF16)
        return carry

    lax.fori_loop(0, members, block, 0)


def project_kernel(place_ref, hidden_ref, scale_ref, *refs):
    weight_refs, out_ref, unit_buf, weight_buf, sems, scale_buf, scale_sem = refs[:8], *refs[8:]
    copies = start_copies(
        [
            [hidden_ref.at[member(place_ref, p // 2, p % 2)] for p in range(8)],
            [weight_refs[p].at[p % 2] for p in range(8)],
        ],
        [unit_buf, weight_buf],
        sems,
    )
    scale_copy = pltpu.make_async_copy(scale_ref, scale_buf, scale_sem)
    scale_copy.start()
    slice_width, wide = weight_refs[0].shape[1:]
    hidden = wide // 3
    slots = out_ref.shape[0] * out_ref.shape[1]
    rows, grads, center = 0.0, 0.0, 0.0
    for place in range(8):
        for copy in copies:
            copy[place].wait()
        units = unit_buf[place, :slots]
        weight = weight_buf[place]
        grads = grads + dot(units[:, : 2 * hidden], weight[:, : 2 * hidden], ((1,), (1,)))
        rows = rows + dot(units[:, 2 * hidden :], weight[:, 2 * hidden :], ((1,), (1,)))
        center = center + unit_buf[place, slots:].astype(F32)
    center = jnp.sum(center, axis=0, keepdims=True)
    center = jnp.broadcast_to(center, (LANES, wide)).T[:slots, :1]
    scale_copy.wait()
    rows, grads, center = rows.astype(BF16), grads.astype(BF16), lanes3(center) + scale_buf[...]
    sources, capacity = out_ref.shape[:2]
    for source in range(sources):
        part = slice(source * capacity, (source + 1) * capacity)
        out_ref[source, :, :slice_width] = rows[part]
        out_ref[source, :, slice_width : 2 * slice_width] = grads[part]
        out_ref[source, :, 2 * slice_width :] = center[part]


def per_device(
    queries,
    latent,
    frames,
    w_uv,
    w_out,
    residual,
    norm_gain,
    expert_ids,
    mix_codes,
    w_gate,
    w_up,
    w_down,
    grad_out,
):
    ctx_count = lax.axis_size("ctx")
    ctx_place = lax.axis_index("ctx")
    plane_x, plane_y = ctx_place // SIDE, ctx_place % SIDE
    group_place = lax.axis_index(GROUP)
    place_z, core = group_place // 2, group_place % 2
    group_count = 8
    token_count = queries.shape[0]
    head_count, latent_width, value_width = w_uv.shape
    model_width = w_gate.shape[1]
    slice_width = residual.shape[1]
    top_count = expert_ids.shape[1]
    hidden_width = w_gate.shape[2]
    column_width = w_out.shape[1]
    capacity = token_count * top_count // ctx_count * 5 // 4
    slot_total = ctx_count * capacity

    def shape(*dims):
        return jax.ShapeDtypeStruct(dims, BF16)

    places = jnp.stack([place_z, core, plane_x, plane_y]).astype(jnp.int32)

    out_weights = [w_out.T]
    out_weights.append(swap_core(w_out.T))
    block = (slice_width, 3 * hidden_width)
    weight_blocks, *weight_pairs = call(
        prepare_kernel, [shape(8, *block)] + [shape(2, *block)] * SIDE, 1
    )(places, w_down[0], w_gate[0], w_up[0])

    chosen = expert_ids.reshape(-1)
    pair_range = jnp.arange(token_count * top_count, dtype=jnp.int32)
    same = (chosen[:, None] == chosen[None, :]) & (pair_range[None, :] < pair_range[:, None])
    earlier = jnp.sum(same.astype(jnp.int32), axis=1)
    slot_index = (chosen * capacity + earlier).reshape(token_count, top_count)
    slot_range = jnp.arange(slot_total, dtype=jnp.int32)
    code_values = mix_codes.astype(F32)
    mix_weight = code_values / jnp.sum(code_values, axis=1, keepdims=True)
    hits = [slot_index[:, k][None, :] == slot_range[:, None] for k in range(top_count)]
    pick = sum(hit.astype(F32) for hit in hits).astype(BF16)
    slot_weight = sum(
        jnp.sum(jnp.where(hits[k], mix_weight[:, k][None, :], 0.0), axis=1) for k in range(top_count)
    )
    returns = [
        (slot_index[:, k][:, None] == slot_range[None, :]).astype(BF16) for k in range(top_count)
    ]

    def to_experts(rows):
        return lax.all_to_all(rows, "ctx", split_axis=0, concat_axis=0, tiled=True)

    grad_rows = (dot(pick, grad_out) * slot_weight[:, None]).astype(BF16)
    grad_rows = to_experts(grad_rows)
    out_grad = group_gather(grad_rows)
    slice_weights = group_exchange(weight_pairs)

    half = token_count // 2
    own_keys = lax.dynamic_slice_in_dim(latent, core * half, half, 0)
    own_frames = lax.dynamic_slice_in_dim(frames, ctx_place * token_count, token_count)
    frame_grid = frames.reshape(SIDE, SIDE, 2, half)
    frame_grid = roll_lead(roll_lead(frame_grid, plane_x, 0), plane_y, 1)
    by_x = jnp.transpose(frame_grid, (2, 0, 1, 3))
    by_y = jnp.transpose(frame_grid, (2, 1, 0, 3))
    key_frames = jnp.where(
        core == 0,
        jnp.concatenate([by_x[0].reshape(-1), by_y[1].reshape(-1)]),
        jnp.concatenate([by_y[1].reshape(-1), by_x[0].reshape(-1)]),
    )
    own_keys = direct_ring(own_keys, 0)
    own_keys, key_frames, own_frames = lax.optimization_barrier(
        (own_keys, key_frames[None], own_frames[:, None])
    )
    own_keys = direct_ring(own_keys, 1)
    own_keys = own_keys.reshape(ctx_count * half, latent_width)
    other_keys = swap_core(own_keys)
    heads = 4
    head_out = pl.pallas_call(
        functools.partial(attend_kernel, latent_width ** (-0.5)),
        out_shape=shape(token_count, head_count * value_width),
        grid=(head_count // heads,),
        in_specs=[
            pl.BlockSpec((token_count, heads * latent_width), lambda h: (0, h)),
            pl.BlockSpec(own_keys.shape, lambda h: (0, 0)),
            pl.BlockSpec(other_keys.shape, lambda h: (0, 0)),
            pl.BlockSpec((1, ctx_count * token_count), lambda h: (0, 0)),
            pl.BlockSpec((token_count, 1), lambda h: (0, 0)),
            pl.BlockSpec((heads, latent_width, value_width), lambda h: (h, 0, 0)),
        ],
        out_specs=pl.BlockSpec((token_count, heads * value_width), lambda h: (0, h)),
        name="attend",
    )(queries, own_keys, other_keys, key_frames, own_frames, w_uv)

    keep = lax.dynamic_slice_in_dim(head_out, core * half, half, 0)
    give = lax.dynamic_slice_in_dim(head_out, (1 - core) * half, half, 0)
    head_part = jnp.stack([keep, swap_core(give)])
    pieces = halves_ring(direct_ring(head_part, 0), 1)
    columns = call(
        out_proj_kernel,
        shape(ctx_count, half, column_width),
        1,
        whole=2,
        scratch_shapes=[pltpu.VMEM(piece.shape, BF16) for piece in pieces]
        + [pltpu.SemaphoreType.DMA((len(pieces),))],
    )(places, *out_weights, *pieces)
    columns = to_experts(columns)
    per_member = ctx_count // group_count
    parts = lax.all_to_all(
        columns.reshape(group_count, per_member * half, column_width), GROUP, 0, 0, tiled=True
    )
    attn_sum = jnp.sum(
        parts.reshape(SIDE, 2, per_member, half, column_width).astype(F32), axis=0
    )
    attn_sum = jnp.transpose(attn_sum, (0, 2, 1, 3)).reshape(token_count, slice_width)
    pre_norm = (residual.astype(F32) + attn_sum).astype(BF16).astype(F32)
    local_gain = lax.dynamic_slice_in_dim(norm_gain, group_place * slice_width, slice_width)
    square = jnp.sum(pre_norm * pre_norm, axis=1, keepdims=True)
    rows_out = jnp.concatenate([(pre_norm * local_gain).astype(BF16), pad_lanes(split3(square))], 1)

    expert_rows = group_gather(to_experts(dot(pick, rows_out).astype(BF16)))
    hidden_send, scaled, slot_scale = call(
        expert_kernel,
        [
            shape(slot_total + 8, 3 * hidden_width),
            shape(slot_total, 2 * hidden_width),
            shape(slot_total, LANES),
        ],
        1,
        0,
        scratch_shapes=buffers(
            (8, slot_total, slice_width + LANES), (8, slot_total, slice_width), (8, *block)
        ),
    )(places, expert_rows, out_grad, weight_blocks)
    hidden_all = group_gather(hidden_send)
    grad_gate, grad_up, grad_down = call(
        weight_grad_kernel,
        [shape(model_width, hidden_width)] * 2 + [shape(hidden_width, model_width)],
    )(expert_rows, out_grad, hidden_send, scaled)
    grad_gate, grad_up, grad_down = grad_gate[None], grad_up[None], grad_down[None]
    back = call(
        project_kernel,
        shape(ctx_count, capacity, 2 * slice_width + LANES),
        1,
        0,
        scratch_shapes=buffers((8, slot_total + 8, 3 * hidden_width), (8, *block))
        + [pltpu.VMEM((slot_total, LANES), BF16), pltpu.SemaphoreType.DMA],
    )(places, hidden_all, slot_scale, *slice_weights)
    back = to_experts(back).reshape(slot_total, 2 * slice_width + LANES)

    picks = [dot(returns[k], back) for k in range(top_count)]
    routed = sum(picks[k][:, :slice_width] * mix_weight[:, k : k + 1] for k in range(top_count))
    layer_out = (pre_norm + routed).astype(BF16)
    summed = sum(pick[:, slice_width : 2 * slice_width] for pick in picks)
    normed_grad = summed.astype(BF16).astype(F32)
    tail = 2 * slice_width
    center = sum(jnp.sum(pick[:, tail : tail + 3], axis=1, keepdims=True) for pick in picks)
    center = center / model_width
    inv_scale = jnp.sum(picks[0][:, tail + 3 : tail + 6], axis=1, keepdims=True)
    scaled_grad = normed_grad * local_gain
    grad_pre_norm = (
        grad_out.astype(F32) + inv_scale * (scaled_grad - pre_norm * inv_scale * center)
    ).astype(BF16)
    return (layer_out, grad_pre_norm, grad_gate, grad_up, grad_down)


def solution(mesh):
    placed = (
        P("ctx", ("role", "exp")),
        P("ctx", None),
        P(),
        P(("role", "exp"), None, None),
        P(("role", "exp"), "ctx"),
        P("ctx", ("role", "exp")),
        P(),
        P("ctx", None),
        P("ctx", None),
        P("ctx", None, ("role", "exp")),
        P("ctx", None, ("role", "exp")),
        P("ctx", ("role", "exp"), None),
        P("ctx", ("role", "exp")),
    )

    return jax.shard_map(
        per_device,
        mesh=mesh,
        in_specs=placed,
        out_specs=(
            P("ctx", ("role", "exp")),
            P("ctx", ("role", "exp")),
            P("ctx", None, ("role", "exp")),
            P("ctx", None, ("role", "exp")),
            P("ctx", ("role", "exp"), None),
        ),
        check_vma=False,
    )
```

```python
import functools

import jax
import jax.numpy as jnp
from jax import lax
from jax.experimental import pallas as pl
from jax.experimental.pallas import tpu as pltpu
from jax.sharding import PartitionSpec as P

ALL = ("ctx", "role", "exp")
GROUP = ("role", "exp")
BF16 = jnp.bfloat16
F32 = jnp.float32
SIDE = 4
LANES = 128


def dot(a, b, dims=((1,), (0,))):
    return lax.dot_general(a, b, (dims, ((), ())), preferred_element_type=F32)


def shift_z(block, step):
    return lax.ppermute(block, GROUP, [(g, (g + 2 * step) % 8) for g in range(8)])


def swap_core(block):
    return lax.ppermute(block, GROUP, [(g, g ^ 1) for g in range(8)])


def shift_plane(block, phase, step):
    pairs = []
    for c in range(SIDE * SIDE):
        x, y = divmod(c, SIDE)
        for g in range(8):
            if g % 2 == phase:
                to = x * SIDE + (y + step) % SIDE
            else:
                to = (x + step) % SIDE * SIDE + y
            pairs.append((c * 8 + g, to * 8 + g))
    return lax.ppermute(block, ALL, pairs)


def direct_ring(block, phase):
    others = [shift_plane(block, phase, -step) for step in range(1, SIDE)]
    return jnp.stack([block] + others)


def halves_ring(block, phase):
    half = block.shape[0] // 2
    before = shift_plane(block, phase, 1)
    after = shift_plane(block, phase, -1)
    far = [shift_plane(before[:half], phase, 1), shift_plane(after[half:], phase, -1)]
    return [block, after, *far, before]


def group_gather(block):
    half = block.shape[0] // 16 * 8
    before = shift_z(block, 1)
    after = shift_z(block, -1)
    near = jnp.stack([block, after, before])
    far = [shift_z(before[:half], 1), shift_z(after[half:], -1)]
    far = jnp.concatenate(far, 0)[None]
    return [near, far, swap_core(near), swap_core(far)]


def blocks_of(refs):
    at = ((0, 0), (0, 1), (1, 0), (0, 2))
    return [refs[2 * other + which].at[n] for which, n in at for other in range(2)]


def group_exchange(blocks):
    received = [
        blocks[0],
        shift_z(blocks[3], -1),
        shift_z(blocks[2], 2),
        shift_z(blocks[1], 1),
    ]
    return [part for pair in received for part in (pair, swap_core(pair))]


def roll_lead(array, shift, axis):
    twice = jnp.concatenate([array, array], axis)
    return lax.dynamic_slice_in_dim(twice, shift, SIDE, axis)


def split3(value):
    high = lax.reduce_precision(value, 8, 7)
    rest = value - high
    middle = lax.reduce_precision(rest, 8, 7)
    low = lax.reduce_precision(rest - middle, 8, 7)
    return [term.astype(BF16) for term in (high, middle, low)]


def pad_lanes(terms):
    rows = terms[0].shape[0]
    blank = jnp.zeros((rows, LANES - len(terms)), BF16)
    return jnp.concatenate([t.reshape(rows, 1) for t in terms] + [blank], 1)


def lanes3(value, kind=BF16, first=0):
    lane = lax.broadcasted_iota(jnp.int32, (value.shape[0], LANES), 1) - first
    high = value.astype(BF16).astype(F32)
    rest = value - high
    middle = rest.astype(BF16).astype(F32)
    low = rest - middle
    wide = jnp.where(lane == 0, high, jnp.where(lane == 1, middle, jnp.where(lane == 2, low, 0.0)))
    return wide.astype(kind)


def call(kernel, outs, scalars=0, whole=None, spaces=None, **params):
    def run(*operands):
        places = [pltpu.SMEM] * scalars
        if spaces is None:
            count = len(operands) - scalars if whole is None else whole
            places += [pltpu.VMEM] * count + [pl.ANY] * (len(operands) - scalars - count)
        else:
            places += spaces
        return pl.pallas_call(
            kernel,
            out_shape=outs,
            in_specs=[pl.BlockSpec(memory_space=space) for space in places],
            **params,
        )(*operands)

    return run


def buffers(*shapes):
    return [pltpu.VMEM(shape, BF16) for shape in shapes] + [
        pltpu.SemaphoreType.DMA((len(shapes), shapes[0][0]))
    ]


def start_copies(lists, bufs, sems):
    for place in range(len(lists[0])):
        for n, (sources, buf) in enumerate(zip(lists, bufs)):
            pltpu.make_async_copy(sources[place], buf.at[place], sems.at[n, place]).start()


def wait_copies(place, lists, bufs, sems):
    for n, (sources, buf) in enumerate(zip(lists, bufs)):
        pltpu.make_async_copy(sources[0], buf.at[place], sems.at[n, place]).wait()


def member(place_ref, step, other):
    z = lax.rem(place_ref[0] + step, SIDE)
    return 2 * z + place_ref[1] + other - 2 * place_ref[1] * other


def prepare_kernel(place_ref, down_ref, gate_ref, up_ref, all_ref, *outs):
    slice_width = all_ref.shape[1]
    hidden = down_ref.shape[0]

    def block(other, carry):
        for step in range(SIDE):
            start = pl.multiple_of(member(place_ref, step, other) * slice_width, LANES)
            gate = gate_ref[pl.ds(start, slice_width), :]
            up = up_ref[pl.ds(start, slice_width), :]
            down = down_ref[:, pl.ds(start, slice_width)].T
            for at, ref in ((2 * step + other, all_ref), (other, outs[step])):
                ref[at, :, :hidden] = gate
                ref[at, :, hidden : 2 * hidden] = up
                ref[at, :, 2 * hidden :] = down
        return carry

    lax.fori_loop(0, 2, block, 0)


def attend_kernel(scale, q_ref, near_ref, far_ref, key_frame_ref, own_frame_ref, uv_ref, out_ref):
    heads, latent_width, value_width = uv_ref.shape
    tokens = q_ref.shape[0]
    keys = [near_ref[...], far_ref[...]]
    count = keys[0].shape[0]
    query = jnp.concatenate(
        [q_ref[:, h * latent_width : (h + 1) * latent_width] for h in range(heads)], 0
    )
    own = own_frame_ref[...]
    scores = []
    for part in range(2):
        visible = key_frame_ref[:, part * count : (part + 1) * count] <= own
        visible = jnp.concatenate([visible.astype(F32)] * heads, 0) > 0.5
        scores.append(jnp.where(visible, dot(query, keys[part], ((1,), (1,))) * scale, -1e30))
    top = jnp.maximum(*[jnp.max(s, axis=1, keepdims=True) for s in scores])
    weights = [jnp.exp(s - top) for s in scores]
    total = sum(jnp.sum(w, axis=1, keepdims=True) for w in weights)
    mix = sum(dot(w.astype(BF16), k) for w, k in zip(weights, keys))
    mix = (mix / total).astype(BF16)
    for h in range(heads):
        out_ref[:, h * value_width : (h + 1) * value_width] = dot(
            mix[h * tokens : (h + 1) * tokens], uv_ref[h]
        ).astype(BF16)


def out_proj_kernel(place_ref, *refs):
    weight_refs, piece_refs, out_ref, *bufs = refs[:2], refs[2:7], *refs[7:]
    piece_bufs, sems = bufs[:5], bufs[5]
    copies = [
        pltpu.make_async_copy(ref, buf, sems.at[n])
        for n, (ref, buf) in enumerate(zip(piece_refs, piece_bufs))
    ]
    for copy in copies:
        copy.start()
    tokens = out_ref.shape[1]
    core = place_ref[1]
    block = 0
    for copy, buf in zip(copies, piece_bufs):
        copy.wait()
        total = 0.0
        for other in range(2):
            rows = buf[:, other].reshape(buf.shape[0] * tokens, buf.shape[3])
            total = total + dot(rows, weight_refs[other][...], ((1,), (1,)))
        total = total.astype(BF16)
        for n in range(buf.shape[0]):
            i, j = block // SIDE, block % SIDE
            step_x = i + core * (j - i)
            step_y = j + core * (i - j)
            owner = lax.rem(place_ref[2] + step_x, SIDE) * SIDE + lax.rem(
                place_ref[3] + step_y, SIDE
            )
            out_ref[owner] = total[n * tokens : (n + 1) * tokens]
            block += 1


def expert_kernel(*refs):
    row_refs, grad_refs, weight_ref, out_ref, scaled_ref, scale_ref, *scratch = (
        refs[:4],
        refs[4:8],
        *refs[8:],
    )
    bufs, sems, both_ref, back_ref, square_ref = scratch[:3], *scratch[3:]
    row_buf, grad_buf, weight_buf = bufs
    lists = [blocks_of(row_refs), blocks_of(grad_refs), [weight_ref.at[p] for p in range(8)]]
    start_copies(lists, bufs, sems)
    hidden = weight_ref.shape[2] // 3
    width = weight_ref.shape[1]
    for ref in (both_ref, back_ref, square_ref):
        ref[...] = jnp.zeros(ref.shape, F32)

    def block(place, carry):
        wait_copies(place, lists, bufs, sems)
        both_ref[...] += dot(row_buf[place, :, :width], weight_buf[place, :, : 2 * hidden])
        back_ref[...] += dot(grad_buf[place], weight_buf[place, :, 2 * hidden :])
        square_ref[...] += row_buf[place, :, width:].astype(F32)
        return carry

    lax.fori_loop(0, 8, block, 0)
    both, hidden_grad, square = both_ref[...], back_ref[...], square_ref[...]
    square = jnp.sum(square, axis=1, keepdims=True)
    inv_scale = lax.rsqrt(square / (8 * width) + 1e-06)
    gate_in, up_in = both[:, :hidden] * inv_scale, both[:, hidden:] * inv_scale
    gate_sig = 1.0 / (1.0 + jnp.exp(-gate_in))
    silu = gate_in * gate_sig
    gate_grad = hidden_grad * up_in * gate_sig * (1.0 + gate_in * (1.0 - gate_sig))
    up_grad = hidden_grad * silu
    center = jnp.sum(gate_grad * gate_in + up_grad * up_in, axis=1, keepdims=True)
    slots = gate_in.shape[0]
    scaled_ref[:, :hidden] = (gate_grad * inv_scale).astype(BF16)
    scaled_ref[:, hidden:] = (up_grad * inv_scale).astype(BF16)
    scale_ref[...] = lanes3(inv_scale, first=3)
    out_ref[:slots, :hidden] = gate_grad.astype(BF16)
    out_ref[:slots, hidden : 2 * hidden] = up_grad.astype(BF16)
    out_ref[:slots, 2 * hidden :] = (silu * up_in).astype(BF16)
    out_ref[slots:, :] = jnp.zeros((out_ref.shape[0] - slots, 3 * hidden), BF16)
    out_ref[slots:, :slots] = lanes3(center, F32).T[: out_ref.shape[0] - slots].astype(BF16)


def weight_grad_kernel(place_ref, *refs):
    row_refs, grad_refs, hidden_ref, scaled_ref = refs[:4], refs[4:8], *refs[8:10]
    gate_ref, up_ref, down_ref, *scratch = refs[10:]
    bufs, sems = scratch[:2], scratch[2]
    lists = [blocks_of(row_refs), blocks_of(grad_refs)]
    start_copies(lists, bufs, sems)
    hidden = gate_ref.shape[1]
    _, slots, slice_width = bufs[1].shape
    grads = scaled_ref[...]
    units = hidden_ref[:slots, 2 * hidden :]

    def block(place, carry):
        wait_copies(place, lists, bufs, sems)
        start = member(place_ref, place // 2, place % 2) * slice_width
        part = pl.ds(pl.multiple_of(start, LANES), slice_width)
        both = dot(bufs[0][place, :, :slice_width], grads, ((0,), (0,)))
        gate_ref[part, :] = both[:, :hidden].astype(BF16)
        up_ref[part, :] = both[:, hidden:].astype(BF16)
        down_ref[:, part] = dot(units, bufs[1][place], ((0,), (0,))).astype(BF16)
        return carry

    lax.fori_loop(0, 8, block, 0)


def project_kernel(*refs):
    hidden_refs, scale_ref, weight_refs, out_ref, *scratch = refs[:4], refs[4], refs[5:13], *refs[13:]
    bufs, sems, scale_buf, scale_sem, rows_acc, grads_acc, center_acc = scratch[:2], *scratch[2:]
    unit_buf, weight_buf = bufs
    lists = [blocks_of(hidden_refs), [weight_refs[p].at[p % 2] for p in range(8)]]
    start_copies(lists, bufs, sems)
    scale_copy = pltpu.make_async_copy(scale_ref, scale_buf, scale_sem)
    scale_copy.start()
    slice_width, wide = weight_refs[0].shape[1:]
    hidden = wide // 3
    slots = out_ref.shape[0] * out_ref.shape[1]
    for ref in (rows_acc, grads_acc, center_acc):
        ref[...] = jnp.zeros(ref.shape, F32)

    def block(place, carry):
        wait_copies(place, lists, bufs, sems)
        units = unit_buf[place, :slots]
        weight = weight_buf[place]
        grads_acc[...] += dot(units[:, : 2 * hidden], weight[:, : 2 * hidden], ((1,), (1,)))
        rows_acc[...] += dot(units[:, 2 * hidden :], weight[:, 2 * hidden :], ((1,), (1,)))
        center_acc[...] += unit_buf[place, slots:].astype(F32)
        return carry

    lax.fori_loop(0, 8, block, 0)
    rows, grads, center = rows_acc[...], grads_acc[...], center_acc[...]
    center = jnp.sum(center, axis=0, keepdims=True)
    center = jnp.broadcast_to(center, (LANES, wide)).T[:slots, :1]
    scale_copy.wait()
    rows, grads, center = rows.astype(BF16), grads.astype(BF16), lanes3(center) + scale_buf[...]
    sources, capacity = out_ref.shape[:2]
    for source in range(sources):
        part = slice(source * capacity, (source + 1) * capacity)
        out_ref[source, :, :slice_width] = rows[part]
        out_ref[source, :, slice_width : 2 * slice_width] = grads[part]
        out_ref[source, :, 2 * slice_width :] = center[part]


def per_device(
    queries,
    latent,
    frames,
    w_uv,
    w_out,
    residual,
    norm_gain,
    expert_ids,
    mix_codes,
    w_gate,
    w_up,
    w_down,
    grad_out,
):
    ctx_count = lax.axis_size("ctx")
    ctx_place = lax.axis_index("ctx")
    plane_x, plane_y = ctx_place // SIDE, ctx_place % SIDE
    group_place = lax.axis_index(GROUP)
    place_z, core = group_place // 2, group_place % 2
    group_count = 8
    token_count = queries.shape[0]
    head_count, latent_width, value_width = w_uv.shape
    model_width = w_gate.shape[1]
    slice_width = residual.shape[1]
    top_count = expert_ids.shape[1]
    hidden_width = w_gate.shape[2]
    column_width = w_out.shape[1]
    capacity = token_count * top_count // ctx_count * 5 // 4
    slot_total = ctx_count * capacity

    def shape(*dims):
        return jax.ShapeDtypeStruct(dims, BF16)

    places = jnp.stack([place_z, core, plane_x, plane_y]).astype(jnp.int32)

    out_weights = [w_out.T]
    out_weights.append(swap_core(w_out.T))
    block = (slice_width, 3 * hidden_width)
    weight_blocks, *weight_pairs = call(
        prepare_kernel, [shape(8, *block)] + [shape(2, *block)] * SIDE, 1
    )(places, w_down[0], w_gate[0], w_up[0])

    chosen = expert_ids.reshape(-1)
    pair_range = jnp.arange(token_count * top_count, dtype=jnp.int32)
    same = (chosen[:, None] == chosen[None, :]) & (pair_range[None, :] < pair_range[:, None])
    earlier = jnp.sum(same.astype(jnp.int32), axis=1)
    slot_index = (chosen * capacity + earlier).reshape(token_count, top_count)
    slot_range = jnp.arange(slot_total, dtype=jnp.int32)
    code_values = mix_codes.astype(F32)
    mix_weight = code_values / jnp.sum(code_values, axis=1, keepdims=True)
    hits = [slot_index[:, k][None, :] == slot_range[:, None] for k in range(top_count)]
    pick = sum(hit.astype(F32) for hit in hits).astype(BF16)
    slot_weight = sum(
        jnp.sum(jnp.where(hits[k], mix_weight[:, k][None, :], 0.0), axis=1) for k in range(top_count)
    )
    returns = [
        (slot_index[:, k][:, None] == slot_range[None, :]).astype(BF16) for k in range(top_count)
    ]

    def to_experts(rows):
        return lax.all_to_all(rows, "ctx", split_axis=0, concat_axis=0, tiled=True)

    grad_rows = (dot(pick, grad_out) * slot_weight[:, None]).astype(BF16)
    grad_rows = to_experts(grad_rows)
    out_grad = group_gather(grad_rows)
    slice_weights = group_exchange(weight_pairs)

    half = token_count // 2
    own_keys = lax.dynamic_slice_in_dim(latent, core * half, half, 0)
    own_frames = lax.dynamic_slice_in_dim(frames, ctx_place * token_count, token_count)
    frame_grid = frames.reshape(SIDE, SIDE, 2, half)
    frame_grid = roll_lead(roll_lead(frame_grid, plane_x, 0), plane_y, 1)
    by_x = jnp.transpose(frame_grid, (2, 0, 1, 3))
    by_y = jnp.transpose(frame_grid, (2, 1, 0, 3))
    key_frames = jnp.where(
        core == 0,
        jnp.concatenate([by_x[0].reshape(-1), by_y[1].reshape(-1)]),
        jnp.concatenate([by_y[1].reshape(-1), by_x[0].reshape(-1)]),
    )
    own_keys = direct_ring(own_keys, 0)
    own_keys, key_frames, own_frames = lax.optimization_barrier(
        (own_keys, key_frames[None], own_frames[:, None])
    )
    own_keys = direct_ring(own_keys, 1)
    own_keys = own_keys.reshape(ctx_count * half, latent_width)
    other_keys = swap_core(own_keys)
    heads = 4
    head_out = pl.pallas_call(
        functools.partial(attend_kernel, latent_width ** (-0.5)),
        out_shape=shape(token_count, head_count * value_width),
        grid=(head_count // heads,),
        in_specs=[
            pl.BlockSpec((token_count, heads * latent_width), lambda h: (0, h)),
            pl.BlockSpec(own_keys.shape, lambda h: (0, 0)),
            pl.BlockSpec(other_keys.shape, lambda h: (0, 0)),
            pl.BlockSpec((1, ctx_count * token_count), lambda h: (0, 0)),
            pl.BlockSpec((token_count, 1), lambda h: (0, 0)),
            pl.BlockSpec((heads, latent_width, value_width), lambda h: (h, 0, 0)),
        ],
        out_specs=pl.BlockSpec((token_count, heads * value_width), lambda h: (0, h)),
        name="attend",
    )(queries, own_keys, other_keys, key_frames, own_frames, w_uv)

    keep = lax.dynamic_slice_in_dim(head_out, core * half, half, 0)
    give = lax.dynamic_slice_in_dim(head_out, (1 - core) * half, half, 0)
    head_part = jnp.stack([keep, swap_core(give)])
    pieces = halves_ring(direct_ring(head_part, 0), 1)
    columns = call(
        out_proj_kernel,
        shape(ctx_count, half, column_width),
        1,
        whole=2,
        scratch_shapes=[pltpu.VMEM(piece.shape, BF16) for piece in pieces]
        + [pltpu.SemaphoreType.DMA((len(pieces),))],
    )(places, *out_weights, *pieces)
    columns = to_experts(columns)
    per_member = ctx_count // group_count
    parts = lax.all_to_all(
        columns.reshape(group_count, per_member * half, column_width), GROUP, 0, 0, tiled=True
    )
    attn_sum = jnp.sum(
        parts.reshape(SIDE, 2, per_member, half, column_width).astype(F32), axis=0
    )
    attn_sum = jnp.transpose(attn_sum, (0, 2, 1, 3)).reshape(token_count, slice_width)
    pre_norm = (residual.astype(F32) + attn_sum).astype(BF16).astype(F32)
    local_gain = lax.dynamic_slice_in_dim(norm_gain, group_place * slice_width, slice_width)
    square = jnp.sum(pre_norm * pre_norm, axis=1, keepdims=True)
    rows_out = jnp.concatenate([(pre_norm * local_gain).astype(BF16), pad_lanes(split3(square))], 1)

    expert_rows = to_experts(dot(pick, rows_out).astype(BF16))
    expert_rows = group_gather(expert_rows)
    hidden_send, scaled, slot_scale = call(
        expert_kernel,
        [
            shape(slot_total + 8, 3 * hidden_width),
            shape(slot_total, 2 * hidden_width),
            shape(slot_total, LANES),
        ],
        0,
        0,
        scratch_shapes=buffers(
            (8, slot_total, slice_width + LANES), (8, slot_total, slice_width), (8, *block)
        )
        + [
            pltpu.VMEM((slot_total, width), F32)
            for width in (2 * hidden_width, hidden_width, LANES)
        ],
    )(*expert_rows, *out_grad, weight_blocks)
    hidden_all = group_gather(hidden_send)
    grad_gate, grad_up, grad_down = call(
        weight_grad_kernel,
        [shape(model_width, hidden_width)] * 2 + [shape(hidden_width, model_width)],
        1,
        spaces=[pl.ANY] * 8 + [pltpu.VMEM] * 2,
        scratch_shapes=buffers(
            (8, slot_total, slice_width + LANES), (8, slot_total, slice_width)
        ),
    )(places, *expert_rows, *out_grad, hidden_send, scaled)
    grad_gate, grad_up, grad_down = grad_gate[None], grad_up[None], grad_down[None]
    back = call(
        project_kernel,
        shape(ctx_count, capacity, 2 * slice_width + LANES),
        0,
        0,
        scratch_shapes=buffers((8, slot_total + 8, 3 * hidden_width), (8, *block))
        + [pltpu.VMEM((slot_total, LANES), BF16), pltpu.SemaphoreType.DMA]
        + [pltpu.VMEM((slot_total, slice_width), F32)] * 2
        + [pltpu.VMEM((8, 3 * hidden_width), F32)],
    )(*hidden_all, slot_scale, *slice_weights)
    back = to_experts(back).reshape(slot_total, 2 * slice_width + LANES)

    picks = [dot(returns[k], back) for k in range(top_count)]
    routed = sum(picks[k][:, :slice_width] * mix_weight[:, k : k + 1] for k in range(top_count))
    layer_out = (pre_norm + routed).astype(BF16)
    summed = sum(pick[:, slice_width : 2 * slice_width] for pick in picks)
    normed_grad = summed.astype(BF16).astype(F32)
    tail = 2 * slice_width
    center = sum(jnp.sum(pick[:, tail : tail + 3], axis=1, keepdims=True) for pick in picks)
    center = center / model_width
    inv_scale = jnp.sum(picks[0][:, tail + 3 : tail + 6], axis=1, keepdims=True)
    scaled_grad = normed_grad * local_gain
    grad_pre_norm = (
        grad_out.astype(F32) + inv_scale * (scaled_grad - pre_norm * inv_scale * center)
    ).astype(BF16)
    return (layer_out, grad_pre_norm, grad_gate, grad_up, grad_down)


def solution(mesh):
    placed = (
        P("ctx", ("role", "exp")),
        P("ctx", None),
        P(),
        P(("role", "exp"), None, None),
        P(("role", "exp"), "ctx"),
        P("ctx", ("role", "exp")),
        P(),
        P("ctx", None),
        P("ctx", None),
        P("ctx", None, ("role", "exp")),
        P("ctx", None, ("role", "exp")),
        P("ctx", ("role", "exp"), None),
        P("ctx", ("role", "exp")),
    )

    return jax.shard_map(
        per_device,
        mesh=mesh,
        in_specs=placed,
        out_specs=(
            P("ctx", ("role", "exp")),
            P("ctx", ("role", "exp")),
            P("ctx", None, ("role", "exp")),
            P("ctx", None, ("role", "exp")),
            P("ctx", ("role", "exp"), None),
        ),
        check_vma=False,
    )
```
